32 devices in a mesh: groups: 2 (over y), sec: 4 (over x, core), tile: 4 (over z).
Axes of the slice: x: 2, y: 2, z: 4, core: 2. Of those that a mesh axis runs over, the one named last changes fastest.
Arguments:
- raw_image: float32 [8, 128, 256], P(('groups', 'sec'), 'tile'), parts along dimension 0, may hold values from -6 to 6
- pairing: int32 [8], P(('groups', 'sec')), parts along dimension 0, may hold values from 0 to 3, as said below
- valid_mask: int32 [8, 4, 8], P(('groups', 'sec'), 'tile'), parts along dimension 0, may hold values 0 or 1
- first_kernel: float32 [32, 1, 3, 3], replicated, may hold values from -2 to 2
- later_kernels: float32 [2, 32, 32, 3, 3], replicated, may hold values from -0.375 to 0.375
- biases: float32 [3, 32], replicated, may hold values from -0.6 to 0.6
Outputs:
- correlation: float32 [8, 4, 8, 289], P(('groups', 'sec'), 'tile'), parts along dimension 0
The draws below stay inside these ranges and needn't reach their ends.
There are 2 independent parts, one for each index of `groups`. The reference program is written for one: setup_inputs(seed, part) draws one part's arguments, and reference() takes and returns one part's arrays. A program takes and returns all parts, laid end to end along the dimension named above; an argument that names none is the same for every part. Nothing has to cross between parts.
Inputs may be any that keep to these rules, and one draw needn't show every extreme that they name: pairing[pairing[s]] = s and pairing[s] is s - 1, s or s + 1; all pairs of one list begin at sections of the same parity, and a section without a partner is paired with itself.
All inputs are finite; a program needn't handle non-finite values. No bound on the sum of `valid_mask` on one device may be relied on, other than what follows from the above.
Results may differ from the reference program's by a relative error of at most 0.0001.
Values sent between devices are 32-bit elements; how exact they have to be, the bound alone decides.
No kernel may reach another device: no remote copies, remote signals or barrier semaphores. Data moves between devices by JAX's collectives and lax.ppermute only.
A program may use at most 128 MiB of HBM per device.

```python
import jax
import jax.numpy as jnp
from jax import lax

C = 32
LAYERS = 3
BLK = 32
RADIUS = 8
W = 256
S = 4
H = 128
NBY = 4
NBX = 8


def draw_pairing(key, part):
    parity = jax.random.randint(jax.random.fold_in(key, 11), (), 0, 2).astype(jnp.int32)
    active = jax.random.randint(jax.random.fold_in(key, 12), (S // 2 + 2,), 0, 4).astype(jnp.int32)
    sections = jnp.arange(S, dtype=jnp.int32)
    slot_index = (sections - parity) // 2
    lower = 2 * slot_index + parity
    higher = lower + 1
    usable = (lower >= 0) & (higher < S) & (active[slot_index + 1] > 0)
    partner = jnp.where(sections == lower, higher, lower)
    return jnp.where(usable, partner, sections).astype(jnp.int32)


def touch_ends(values, key, smallest, largest):
    place = [jax.random.randint(jax.random.fold_in(key, axis), (), 0, length) for axis, length in enumerate(values.shape)]
    main_axis = values.shape.index(max(values.shape))
    next_to = place[:main_axis] + [(place[main_axis] + 1) % values.shape[main_axis]] + place[main_axis + 1:]
    return values.at[tuple(place)].set(smallest).at[tuple(next_to)].set(largest)


def shard_levels(stream_key, extent, pieces, least, largest):
    loudness, own = 1.0, jax.random.fold_in(stream_key, 6)
    for dim, parts in pieces:
        heights = jnp.exp(jax.random.uniform(jax.random.fold_in(own, dim), (parts,), jnp.float32, least / len(pieces), largest / len(pieces)))
        loudness = loudness * jnp.repeat(heights, extent[dim] // parts).reshape([-1 if axis == dim else 1 for axis in range(len(extent))])
    return loudness


def normal_values(stream_key, dims, scale, most, cuts=(), kind=jnp.bfloat16):
    level = shard_levels(stream_key, dims, cuts, -0.22, 0.18) if cuts else 1.0
    result = jax.random.normal(stream_key, dims, jnp.float32) * scale * level
    return jnp.minimum(jnp.maximum(result, -most), most).astype(kind)


def setup_inputs(seed: int = 0, part: int = 0) -> dict:
    splits = jax.random.split(jax.random.key(seed), 7)
    own_keys = jax.random.split(jax.random.fold_in(splits[6], part), 7)
    raw_image = normal_values(own_keys[0], (S, H, W), 1.0, 6.0, ((0, 4), (1, 4)), jnp.float32)
    pairing = draw_pairing(jax.random.fold_in(jax.random.fold_in(splits[6], part), 71), part)
    valid_mask = touch_ends((jax.random.randint(own_keys[2], (S, NBY, NBX), 0, 4) < 3).astype(jnp.int32), jax.random.fold_in(own_keys[2], 1), 0, 1)
    first_kernel = normal_values(splits[3], (C, 1, 3, 3), 9 ** -0.5, 2.0, (), jnp.float32)
    later_kernels = normal_values(splits[4], (LAYERS - 1, C, C, 3, 3), (9 * C) ** -0.5, 0.375, (), jnp.float32)
    biases = normal_values(splits[5], (LAYERS, C), 0.1, 0.6, (), jnp.float32)
    return dict(raw_image=raw_image, pairing=pairing, valid_mask=valid_mask, first_kernel=first_kernel, later_kernels=later_kernels, biases=biases)


def encode(single, first_kernel, later_kernels, biases):
    current = single[None, None]
    for layer in range(LAYERS):
        kernel = first_kernel if layer == 0 else later_kernels[layer - 1]
        current = lax.conv_general_dilated(current, kernel, (1, 1), ((1, 1), (1, 1)), dimension_numbers=('NCHW', 'OIHW', 'NCHW'), precision=lax.Precision.HIGHEST)
        current = current + biases[layer][None, :, None, None]
        if layer < LAYERS - 1:
            current = jnp.tanh(current)
    return current[0]

def correlate(own_feats, padded):
    channels, strip_rows, width = own_feats.shape
    block_rows = strip_rows // BLK
    block_cols = width // BLK
    span = BLK + 2 * RADIUS
    widened = jnp.pad(padded, ((0, 0), (0, 0), (RADIUS, BLK - RADIUS)))
    leading = widened[:, :, :width].reshape(channels, strip_rows + 2 * RADIUS, block_cols, BLK)
    second = widened[:, :, BLK:BLK + width].reshape(channels, strip_rows + 2 * RADIUS, block_cols, BLK)[..., :2 * RADIUS]
    windows = jnp.concatenate([leading, second], axis=-1).reshape(channels, strip_rows + 2 * RADIUS, block_cols * span)
    blocks = own_feats.reshape(channels, block_rows, BLK, block_cols, BLK)
    column = jnp.arange(BLK, dtype=jnp.int32)[:, None, None]
    target = jnp.arange(span, dtype=jnp.int32)[None, :, None]
    moved = jnp.arange(2 * RADIUS + 1, dtype=jnp.int32)[None, None, :]
    picker = (target == column + moved).astype(jnp.float32)

    def one_shift(offset):
        strip_band = lax.dynamic_slice_in_dim(windows, offset, strip_rows, 1)
        strip_band = strip_band.reshape(channels, block_rows, BLK, block_cols, span)
        products = jnp.einsum('cnybx,cnybz->nbxz', blocks, strip_band, precision=lax.Precision.HIGHEST)
        return jnp.einsum('nbxz,xzd->nbd', products, picker, precision=lax.Precision.HIGHEST)
    shifted = lax.map(one_shift, jnp.arange(2 * RADIUS + 1, dtype=jnp.int32))
    shifted = jnp.transpose(shifted, (1, 2, 0, 3)).reshape(block_rows, block_cols, (2 * RADIUS + 1) ** 2)
    return shifted / jnp.sqrt(jnp.float32(BLK * BLK * channels))

def reference(raw_image, pairing, valid_mask, first_kernel, later_kernels, biases):
    features = lax.map(lambda single: encode(single, first_kernel, later_kernels, biases), raw_image)

    def one_section(which):
        own_feats = lax.dynamic_index_in_dim(features, which, 0, keepdims=False)
        partner = lax.dynamic_index_in_dim(features, pairing[which], 0, keepdims=False)
        padded = jnp.pad(partner, ((0, 0), (RADIUS, RADIUS), (0, 0)))
        weights = lax.dynamic_index_in_dim(valid_mask, which, 0, keepdims=False).astype(jnp.float32)
        return correlate(own_feats, padded) * weights[:, :, None]
    return lax.map(one_section, jnp.arange(S, dtype=jnp.int32))
```

```python
import functools

import jax
import jax.numpy as jnp
import numpy as np
from jax import lax
from jax.experimental import pallas as pl
from jax.experimental.pallas import tpu as pltpu
from jax.sharding import PartitionSpec as P

LAYERS = 3
BLK = 32
RADIUS = 8
C = 32
SHIFTS = 2 * RADIUS + 1
HALO = RADIUS + LAYERS
RAW_ROWS = 64
GROUP = 6
LANES = 128
bf16 = jnp.bfloat16
f32 = jnp.float32


def pairs_even(n):
    return [(i, i ^ 1) for i in range(n) if (i ^ 1) < n]


def pairs_odd(n):
    return [(i, ((i + 1) ^ 1) - 1) for i in range(n) if 0 <= ((i + 1) ^ 1) - 1 < n]


def split(value):
    high = value.astype(bf16)
    return high, (value - high.astype(f32)).astype(bf16)


def dot(left, right):
    return jnp.dot(left, right, preferred_element_type=f32)


def kernel(
    info, own_ref, even_ref, odd_ref, wc_ref, bias_ref, out_ref,
    t1, t2h, t2l, t3h, t3l, raw, x1h, x1l, x2h, x2l, x3h, x3l, bh, bl, ah, al,
):
    width = 256
    iota = lambda shape, axis: lax.broadcasted_iota(jnp.int32, shape, axis)
    tile, tiles, section, pair = info[0], info[1], info[2], info[3]

    lane = iota((C, LANES), 1)
    first = wc_ref[2 * 96:2 * 96 + C, :]
    for yo in range(8):
        rolled = pltpu.roll(first, yo, 1) if yo else first
        high, low = split(rolled)
        rows = slice(yo * C, (yo + 1) * C)
        t1[rows, 0:48] = high[:, 0:48]
        t1[rows, 48:96] = low[:, 0:48]
        t1[rows, 96:144] = high[:, 0:48]
    for layer, (th, tl) in enumerate(((t2h, t2l), (t3h, t3l))):
        for kx in range(3):
            piece = wc_ref[layer * 96 + kx * C:layer * 96 + (kx + 1) * C, :]
            wide = jnp.concatenate([piece, jnp.zeros((C, LANES), f32)], axis=1)
            for yo in range(GROUP):
                rolled = pltpu.roll(wide, yo * C, 1) if yo else wide
                high, low = split(rolled)
                rows = slice((kx * GROUP + yo) * C, (kx * GROUP + yo + 1) * C)
                th[rows, :] = high
                tl[rows, :] = low

    own = own_ref[...]
    partner = jnp.where(pair == section, own, jnp.where(pair == (section ^ 1), even_ref[...], odd_ref[...]))
    col = iota((RAW_ROWS, width), 1)
    for which, image in enumerate((own, partner)):
        raw[which, 0] = jnp.where(col == 0, 0.0, pltpu.roll(image, 1, 1))
        raw[which, 1] = image
        raw[which, 2] = jnp.where(col == width - 1, 0.0, pltpu.roll(image, width - 1, 1))

    plan = ((0, 8, 5, 6, 6, 0, 0), (1, 0, 7, 9, 8, 0, 0))
    edge = iota((C, width), 1)

    def conv(th, tl, xh, xl, group, bias):
        rows = slice(group * GROUP * C, (group * GROUP + 8) * C)
        th, tl, xh, xl = th[...], tl[...], xh[rows, :], xl[rows, :]
        r = dot(jnp.concatenate([th, tl, th], 1), jnp.concatenate([xh, xh, xl], 0))
        n = GROUP * C
        outs = []
        for yo in range(GROUP):
            a = r[yo * C:(yo + 1) * C]
            b = r[n + yo * C:n + (yo + 1) * C]
            c = r[2 * n + yo * C:2 * n + (yo + 1) * C]
            a = jnp.where(edge == 0, 0.0, pltpu.roll(a, 1, 1))
            c = jnp.where(edge == width - 1, 0.0, pltpu.roll(c, width - 1, 1))
            outs.append(a + b + c + bias)
        return outs

    def zero(refs, first_row, last_row):
        for ref in refs:
            ref[first_row * C:last_row * C, :] = jnp.zeros(((last_row - first_row) * C, width), bf16)

    for which in range(2):
        if which == 0:
            base, g1, g2, g3 = 8, 5, 6, 6
            top1, top2, end1, end2 = 2, 1, 34, 33
            o3h, o3l = x3h, x3l
        else:
            base, g1, g2, g3 = 0, 7, 9, 8
            top1, top2, end1, end2 = 10, 9, 42, 41
            o3h, o3l = bh, bl
        bias1 = jnp.broadcast_to(bias_ref[0:C, 0:1], (C, width))
        bias2 = jnp.broadcast_to(bias_ref[0:C, 1:2], (C, width))
        bias3 = jnp.broadcast_to(bias_ref[0:C, 2:3], (C, width))
        for g in range(g1):
            parts = [raw[which, kx, base + 8 * g:base + 8 * g + 16, :] for kx in range(3)]
            high, low = split(jnp.concatenate(parts, 0))
            r = dot(t1[...], jnp.concatenate([high, high, low], 0))
            for yo in range(8):
                high, low = split(jnp.tanh(r[yo * C:(yo + 1) * C] + bias1))
                rows = slice((8 * g + yo) * C, (8 * g + yo + 1) * C)
                x1h[rows, :] = high
                x1l[rows, :] = low
        n1, n2 = 8 * g1, GROUP * g2

        @pl.when(tile == 0)
        def _():
            zero((x1h, x1l), 0, top1)

        @pl.when(tile == tiles - 1)
        def _():
            zero((x1h, x1l), end1, n1)

        for g in range(g2):
            for yo, value in enumerate(conv(t2h, t2l, x1h, x1l, g, bias2)):
                high, low = split(jnp.tanh(value))
                rows = slice((GROUP * g + yo) * C, (GROUP * g + yo + 1) * C)
                x2h[rows, :] = high
                x2l[rows, :] = low
        if which == 0:
            zero((x2h, x2l), 36, 38)

        @pl.when(tile == 0)
        def _():
            zero((x2h, x2l), 0, top2)

        @pl.when(tile == tiles - 1)
        def _():
            zero((x2h, x2l), end2, n2)

        for g in range(g3):
            for yo, value in enumerate(conv(t3h, t3l, x2h, x2l, g, bias3)):
                high, low = split(value)
                rows = slice((GROUP * g + yo) * C, (GROUP * g + yo + 1) * C)
                o3h[rows, :] = high
                o3l[rows, :] = low

    @pl.when(tile == 0)
    def _():
        zero((bh, bl), 0, 8)

    @pl.when(tile == tiles - 1)
    def _():
        zero((bh, bl), 40, 48)

    n = BLK * C
    ah[...] = jnp.transpose(x3h[0:n, :])
    al[...] = jnp.transpose(x3l[0:n, :])
    left = jnp.concatenate([ah[...], al[...], ah[...]], 1)
    lane8 = iota((8, LANES), 1)
    sub8 = iota((8, LANES), 0)
    weight = jnp.zeros((8, LANES), f32)
    for b in range(8):
        weight = jnp.where(sub8 == b, info[4 + b].astype(f32), weight)
    weight = weight * np.float32(1.0 / np.sqrt(BLK * BLK * C))
    total = jnp.zeros((8, 3 * LANES), f32)
    for dy in range(SHIFTS):
        rows = slice(dy * C, dy * C + n)
        high = bh[rows, :]
        p = dot(left, jnp.concatenate([high, high, bl[rows, :]], 0))
        sums = []
        for b in range(8):
            acc = None
            for j in range(4):
                start = BLK * b - RADIUS + 8 * j
                v = p[BLK * b + 8 * j:BLK * b + 8 * j + 8, :]
                v = pltpu.roll(v, (width - start) % width, 1)[:, :LANES] if start else v[:, :LANES]
                if start < 0:
                    v = jnp.where(lane8 < -start, 0.0, v)
                if start + 24 > width:
                    v = jnp.where(lane8 >= width - start, 0.0, v)
                acc = v if acc is None else acc + v
            for bit in (1, 2, 4):
                acc = jnp.where((sub8 & bit) != 0, pltpu.roll(acc, LANES - bit, 1), acc)
            sums.append(jnp.sum(acc, axis=0, keepdims=True))
        d = jnp.where(lane8 < SHIFTS, jnp.concatenate(sums, 0), 0.0)
        d = jnp.concatenate([d, jnp.zeros((8, 2 * LANES), f32)], 1)
        total = total + (pltpu.roll(d, SHIFTS * dy, 1) if dy else d)
    total = total * jnp.concatenate([weight] * 3, 1)
    out_ref[...] = total[:, :SHIFTS * SHIFTS]


def call_kernel(info, own, even, odd, compact, bias):
    width = own.shape[-1]
    vmem = pl.BlockSpec(memory_space=pltpu.VMEM)
    buf = lambda rows: pltpu.VMEM((rows * C, width), bf16)
    return pl.pallas_call(
        kernel,
        out_shape=jax.ShapeDtypeStruct((8, SHIFTS * SHIFTS), f32),
        in_specs=[pl.BlockSpec(memory_space=pltpu.SMEM)] + [vmem] * 5,
        out_specs=vmem,
        scratch_shapes=[
            pltpu.VMEM((256, 144), bf16),
            pltpu.VMEM((576, 256), bf16), pltpu.VMEM((576, 256), bf16),
            pltpu.VMEM((576, 256), bf16), pltpu.VMEM((576, 256), bf16),
            pltpu.VMEM((2, 3, RAW_ROWS, width), f32),
            buf(56), buf(56), buf(54), buf(54), buf(36), buf(36), buf(48), buf(48),
            pltpu.VMEM((width, BLK * C), bf16), pltpu.VMEM((width, BLK * C), bf16),
        ],
        compiler_params=pltpu.CompilerParams(vmem_limit_bytes=48 << 20),
        name="correlate",
    )(info, own, even, odd, compact, bias)


def body(raw_image, pairing, valid_mask, first_kernel, later_kernels, biases):
    tiles, sections = lax.axis_size("tile"), lax.axis_size("sec")
    tile, section = lax.axis_index("tile"), lax.axis_index("sec")
    image = raw_image[0]
    rows, width = image.shape
    odd_tile = (tile % 2) == 1
    top, bottom = image[:HALO], image[rows - HALO:]
    got_even = lax.ppermute(jnp.where(odd_tile, top, bottom), "tile", pairs_even(tiles))
    got_odd = lax.ppermute(jnp.where(odd_tile, bottom, top), "tile", pairs_odd(tiles))
    above = jnp.where(odd_tile, got_even, got_odd)
    below = jnp.where(odd_tile, got_odd, got_even)
    own = jnp.concatenate([above, image, below, jnp.zeros((RAW_ROWS - rows - 2 * HALO, width), f32)], 0)
    even = lax.ppermute(own, "sec", pairs_even(sections))
    odd = lax.ppermute(own, "sec", pairs_odd(sections))

    later = jnp.transpose(later_kernels, (0, 4, 1, 3, 2)).reshape(2 * 3 * C, 3 * C)
    later = jnp.pad(later, ((0, 0), (0, LANES - 3 * C)))
    first = jnp.pad(jnp.transpose(first_kernel[:, 0], (0, 2, 1)), ((0, 0), (0, 0), (0, 13))).reshape(C, 48)
    first = jnp.pad(first, ((0, 0), (0, LANES - 48)))
    compact = jnp.concatenate([later, first], 0)
    info = jnp.concatenate([
        jnp.stack([tile, jnp.int32(tiles), section, pairing[0]]).astype(jnp.int32),
        valid_mask.reshape(-1),
    ])
    result = call_kernel(info, own, even, odd, compact, jnp.transpose(biases))
    return result[None, None]


def solution(mesh):
    placed = (
        P(("groups", "sec"), "tile", None),
        P(("groups", "sec")),
        P(("groups", "sec"), "tile", None),
        P(),
        P(),
        P(),
    )
    return jax.shard_map(
        body,
        mesh=mesh,
        in_specs=placed,
        out_specs=P(("groups", "sec"), "tile", None, None),
        check_vma=False,
    )
```

```python
import jax
import jax.numpy as jnp
import numpy as np
from jax import lax
from jax.experimental import pallas as pl
from jax.experimental.pallas import tpu as pltpu
from jax.sharding import PartitionSpec as P

LAYERS = 3
BLK = 32
RADIUS = 8
C = 32
SHIFTS = 2 * RADIUS + 1
HALO = RADIUS + LAYERS
RAW_ROWS = 64
GROUP = 6
LANES = 128
WIDTH = 256
WIN = 64
SPAN = WIN + 2 * RADIUS
JOINT = 4
STEPS = 5
DEEP = (BLK + JOINT) * C
BAND = 24
bf16 = jnp.bfloat16
f32 = jnp.float32


def pairs_even(n):
    return [(i, i ^ 1) for i in range(n) if (i ^ 1) < n]


def pairs_odd(n):
    return [(i, ((i + 1) ^ 1) - 1) for i in range(n) if 0 <= ((i + 1) ^ 1) - 1 < n]


def split(value):
    high = value.astype(bf16)
    return high, (value - high.astype(f32)).astype(bf16)


def dot(left, right):
    return jnp.dot(left, right, preferred_element_type=f32)


def iota(shape, axis):
    return lax.broadcasted_iota(jnp.int32, shape, axis)


def prepare(later_ref, first_ref, bias_ref, image_ref, t1, t2, t3, spread, image):
    image[...] = image_ref[...]
    for layer, t in enumerate((t2, t3)):
        for kx in range(3):
            taps = [later_ref[layer, ky, kx] for ky in range(3)]
            wide = jnp.concatenate(taps + [jnp.zeros((C, LANES - 3 * C), f32)], axis=1)
            wide = jnp.concatenate([wide, jnp.zeros((C, LANES), f32)], axis=1)
            for yo in range(GROUP):
                high, low = split(pltpu.roll(wide, yo * C, 1) if yo else wide)
                rows = slice((kx * GROUP + yo) * C, (kx * GROUP + yo + 1) * C)
                t[0, rows, :] = high
                t[1, rows, :] = low
    taps = first_ref[...]
    taps = jnp.concatenate([taps] * (WIDTH // C), axis=1)
    offset = iota((16, WIDTH), 0) - iota((16, WIDTH), 1) // C
    pieces = []
    for kx in range(3):
        piece = jnp.zeros((16, WIDTH), f32)
        for ky in range(3):
            row = taps[3 * ky + kx:3 * ky + kx + 1, :]
            piece = jnp.where(offset == ky, jnp.broadcast_to(row, (16, WIDTH)), piece)
        pieces.append(piece)
    pieces.append(jnp.zeros((LANES - 48, WIDTH), f32))
    high, low = split(jnp.transpose(jnp.concatenate(pieces, 0)))
    t1[:, 0:48] = high[:, 0:48]
    t1[:, 48:96] = low[:, 0:48]
    t1[:, 96:144] = high[:, 0:48]
    b = jnp.concatenate([bias_ref[...], jnp.zeros((LAYERS, LANES - C), f32)], 1)
    b = jnp.transpose(jnp.concatenate([b, jnp.zeros((8 - LAYERS, LANES), f32)], 0))
    for layer in range(LAYERS):
        spread[layer] = jnp.broadcast_to(b[0:C, layer:layer + 1], (C, WIDTH))


def encode(image, base, groups, ends, tile, tiles, t1, t2, t3, spread, raw, x1, x2, emit):
    n1, n2 = 8 * groups[0], GROUP * groups[1]
    col = iota((RAW_ROWS, WIDTH), 1)
    raw[0] = jnp.where(col == 0, 0.0, pltpu.roll(image, 1, 1))
    raw[1] = image
    raw[2] = jnp.where(col == WIDTH - 1, 0.0, pltpu.roll(image, WIDTH - 1, 1))
    edge = iota((C, WIDTH), 1)

    def put(x, row, value):
        high, low = split(value)
        x[0, row * C:(row + 1) * C, :] = high
        x[1, row * C:(row + 1) * C, :] = low

    def outside(x, top, end, rows):
        @pl.when(tile == 0)
        def _():
            x[:, 0:top * C, :] = jnp.zeros((2, top * C, WIDTH), bf16)

        @pl.when(tile == tiles - 1)
        def _():
            x[:, end * C:rows * C, :] = jnp.zeros((2, (rows - end) * C, WIDTH), bf16)

    def conv(t, x, group, bias):
        rows = slice(group * GROUP * C, (group * GROUP + 8) * C)
        th, tl, xh, xl = t[0], t[1], x[0, rows, :], x[1, rows, :]
        r = dot(jnp.concatenate([th, tl, th], 1), jnp.concatenate([xh, xh, xl], 0))
        n = GROUP * C
        for yo in range(GROUP):
            a = r[yo * C:(yo + 1) * C]
            b = r[n + yo * C:n + (yo + 1) * C]
            c = r[2 * n + yo * C:2 * n + (yo + 1) * C]
            a = jnp.where(edge == 0, 0.0, pltpu.roll(a, 1, 1))
            c = jnp.where(edge == WIDTH - 1, 0.0, pltpu.roll(c, WIDTH - 1, 1))
            yield group * GROUP + yo, a + b + c + bias

    for g in range(groups[0]):
        parts = [raw[kx, base + 8 * g:base + 8 * g + 16, :] for kx in range(3)]
        high, low = split(jnp.concatenate(parts, 0))
        r = dot(t1[...], jnp.concatenate([high, high, low], 0))
        for yo in range(8):
            put(x1, 8 * g + yo, jnp.tanh(r[yo * C:(yo + 1) * C] + spread[0]))
    outside(x1, ends[0], ends[1], n1)
    for g in range(groups[1]):
        for row, value in conv(t2, x1, g, spread[1]):
            put(x2, row, jnp.tanh(value))
    outside(x2, ends[2], ends[3], n2)
    for row in range(n2, GROUP * groups[2] + 2):
        x2[:, row * C:(row + 1) * C, :] = jnp.zeros((2, C, WIDTH), bf16)
    for g in range(groups[2]):
        for row, value in conv(t3, x2, g, spread[2]):
            emit(row, value)


def own_features(where, image_ref, t1, t2, t3, spread, packed, raw, x1, x2, kept):
    tile, tiles = where[0], where[1]
    pad = JOINT - 1
    kept[:, :, 0:pad * C, :] = jnp.zeros((2, 2, pad * C, WIDTH), bf16)
    kept[:, :, (pad + BLK) * C:, :] = jnp.zeros((2, 2, JOINT * C, WIDTH), bf16)

    def emit(row, value):
        if row >= BLK:
            return
        turned = [pltpu.roll(value[:, i:i + LANES], WIN, 1) for i in range(0, WIDTH, LANES)]
        rows = slice((row + pad) * C, (row + pad + 1) * C)
        for form, v in enumerate((value, jnp.concatenate(turned, 1))):
            kept[form, 0, rows, :], kept[form, 1, rows, :] = split(v)

    encode(image_ref[...], RADIUS, (5, 6, 6), (2, 34, 1, 33), tile, tiles,
           t1, t2, t3, spread, raw, x1, x2, emit)
    left = iota((C, LANES), 1) < WIN
    for w in range(WIDTH // WIN):
        half = slice((w // 2) * LANES, (w // 2 + 1) * LANES)
        for part in range(2):
            for y in range(BLK + JOINT):
                cols = []
                for g in (0, 2):
                    a = kept[w % 2, part, (y - g + pad) * C:(y - g + pad + 1) * C, half]
                    b = kept[1 - w % 2, part, (y - g - 1 + pad) * C:(y - g + pad) * C, half]
                    cols.append(jnp.where(left, a, b))
                packed[w, part, y * C:(y + 1) * C, :] = jnp.concatenate(cols, 1)


def correlate(where, pair, mask, own_ref, even_ref, odd_ref, t1, t2, t3, spread, packed, out_ref,
              raw, x1, x2, feats, turned):
    tile, tiles, section = where[0], where[1], where[2]
    image = jnp.where(pair[0] == section, own_ref[...],
                      jnp.where(pair[0] == (section ^ 1), even_ref[...], odd_ref[...]))

    def emit(row, value):
        feats[row * C:(row + 1) * C, :] = value

    encode(image, 0, (7, 9, 8), (10, 42, 9, 41), tile, tiles, t1, t2, t3, spread, raw, x1, x2, emit)

    @pl.when(tile == 0)
    def _():
        feats[0:RADIUS * C, :] = jnp.zeros((RADIUS * C, WIDTH), f32)

    @pl.when(tile == tiles - 1)
    def _():
        feats[(BLK + RADIUS) * C:, :] = jnp.zeros((RADIUS * C, WIDTH), f32)

    border = jnp.zeros((RADIUS, LANES), f32)
    turned[:, :, (BLK + 2 * RADIUS) * C:] = jnp.zeros((2, WIDTH + 2 * RADIUS, JOINT * C), bf16)
    for q in range((BLK + 2 * RADIUS) * C // LANES):
        cols = slice(q * LANES, (q + 1) * LANES)
        v = jnp.concatenate([border, jnp.transpose(feats[cols, :]), border], 0)
        turned[0, :, cols], turned[1, :, cols] = split(v)

    lane8, sub8 = iota((8, LANES), 1), iota((8, LANES), 0)
    eighth = (iota((8, WIDTH), 1) % WIN) // 8
    sums = [[None] * 8 for _ in range(JOINT)]
    for w in range(WIDTH // WIN):
        rows = slice(w * WIN, w * WIN + SPAN)
        lefts = []
        for j in range(STEPS):
            cols = slice(j * JOINT * C, j * JOINT * C + DEEP)
            high, low = turned[0, rows, cols], turned[1, rows, cols]
            lefts.append(jnp.concatenate([high, low, high], 1))
        right = jnp.concatenate([packed[w, 0], packed[w, 0], packed[w, 1]], 0)
        p = dot(jnp.concatenate(lefts, 0), right)
        bands = []
        for j in range(STEPS):
            for k in range(3):
                band = None
                for m in range(8):
                    start = j * SPAN + 8 * (m + k)
                    v = p[start:start + 8, :]
                    band = v if band is None else jnp.where(eighth == m, v, band)
                bands.append(band)
        bands.append(jnp.zeros((8, WIDTH), f32))
        flat = jnp.transpose(jnp.concatenate(bands, 0))
        for g in range(JOINT):
            for side in range(2):
                at = g * WIN + side * BLK
                v = flat[at:at + 8] + flat[at + 8:at + 16] + flat[at + 16:at + 24] + flat[at + 24:at + 32]
                for bit in (1, 2, 4):
                    v = jnp.where((sub8 & bit) != 0, pltpu.roll(v, LANES - bit, 1), v)
                sums[g][2 * w + side] = jnp.sum(v, axis=0, keepdims=True)
    total = jnp.zeros((8, 3 * LANES), f32)
    lane = iota((8, 3 * LANES), 1)
    for g in range(JOINT):
        d = jnp.concatenate(sums[g], 0)
        d = jnp.concatenate([d, jnp.zeros((8, 2 * LANES), f32)], 1)
        for j in range(STEPS):
            dy = JOINT * j + g
            if dy < SHIFTS:
                shift = (SHIFTS * dy - BAND * j) % (3 * LANES)
                here = (lane >= SHIFTS * dy) & (lane < SHIFTS * (dy + 1))
                total = jnp.where(here, pltpu.roll(d, shift, 1) if shift else d, total)
    weight = jnp.zeros((8, 3 * LANES), f32)
    for b in range(8):
        weight = jnp.where(iota((8, 3 * LANES), 0) == b, mask[b].astype(f32), weight)
    total = total * (weight * np.float32(1.0 / np.sqrt(BLK * BLK * C)))
    out_ref[...] = total[:, :SHIFTS * SHIFTS]


VMEM = pl.BlockSpec(memory_space=pltpu.VMEM)
SMEM = pl.BlockSpec(memory_space=pltpu.SMEM)


def params(flops, moved):
    return dict(
        compiler_params=pltpu.CompilerParams(vmem_limit_bytes=40 << 20),
        cost_estimate=pl.CostEstimate(flops=flops, bytes_accessed=moved, transcendentals=0),
    )


def scratch(rows1, rows2):
    return [
        pltpu.VMEM((3, RAW_ROWS, WIDTH), f32),
        pltpu.VMEM((2, rows1 * C, WIDTH), bf16),
        pltpu.VMEM((2, rows2 * C, WIDTH), bf16),
    ]


def body(raw_image, pairing, valid_mask, first_kernel, later_kernels, biases):
    tiles, sections = lax.axis_size("tile"), lax.axis_size("sec")
    tile, section = lax.axis_index("tile"), lax.axis_index("sec")
    image = raw_image[0]
    rows, width = image.shape
    shape = jax.ShapeDtypeStruct
    got_even = lax.ppermute(image, "tile", pairs_even(tiles))
    got_odd = lax.ppermute(image, "tile", pairs_odd(tiles))
    t1, t2, t3, spread, image = pl.pallas_call(
        prepare,
        out_shape=[shape((256, 144), bf16), shape((2, 576, 256), bf16), shape((2, 576, 256), bf16),
                   shape((LAYERS, C, WIDTH), f32), shape(image.shape, f32)],
        in_specs=[VMEM] * 4, out_specs=[VMEM] * 5, name="prepare", **params(10**6, 3 * 10**6),
    )(jnp.transpose(later_kernels, (0, 3, 4, 1, 2)),
      jnp.transpose(first_kernel, (2, 3, 1, 0)).reshape(9, C), biases, image)

    odd_tile = (tile % 2) == 1
    above = jnp.where(odd_tile, got_even[rows - HALO:], got_odd[rows - HALO:])
    below = jnp.where(odd_tile, got_odd[:HALO], got_even[:HALO])
    own = jnp.concatenate([above, image, below, jnp.zeros((RAW_ROWS - rows - 2 * HALO, width), f32)], 0)
    even = lax.ppermute(own, "sec", pairs_even(sections))
    odd = lax.ppermute(own, "sec", pairs_odd(sections))
    where = jnp.stack([tile, jnp.int32(tiles), section]).astype(jnp.int32)
    packed = pl.pallas_call(
        own_features,
        out_shape=shape((WIDTH // WIN, 2, DEEP, WIDTH), bf16),
        in_specs=[SMEM] + [VMEM] * 5, out_specs=VMEM,
        scratch_shapes=scratch(40, 38) + [pltpu.VMEM((2, 2, (BLK + 2 * JOINT - 1) * C, WIDTH), bf16)],
        name="own_features", **params(5 * 10**9, 10**7),
    )(where, own, t1, t2, t3, spread)
    result = pl.pallas_call(
        correlate,
        out_shape=shape((8, SHIFTS * SHIFTS), f32),
        in_specs=[SMEM] * 3 + [VMEM] * 8, out_specs=VMEM,
        scratch_shapes=scratch(56, 54) + [
            pltpu.VMEM(((BLK + 2 * RADIUS) * C, WIDTH), f32),
            pltpu.VMEM((2, WIDTH + 2 * RADIUS, (BLK + 2 * RADIUS + JOINT) * C), bf16),
        ],
        name="correlate", **params(10**10, 10**7),
    )(where, pairing, valid_mask.reshape(-1), own, even, odd, t1, t2, t3, spread, packed)
    return result[None, None]


def solution(mesh):
    placed = (
        P(("groups", "sec"), "tile", None),
        P(("groups", "sec")),
        P(("groups", "sec"), "tile", None),
        P(),
        P(),
        P(),
    )
    return jax.shard_map(
        body,
        mesh=mesh,
        in_specs=placed,
        out_specs=P(("groups", "sec"), "tile", None, None),
        check_vma=False,
    )
```

```python
import jax
import jax.numpy as jnp
import numpy as np
from jax import lax
from jax.experimental import pallas as pl
from jax.experimental.pallas import tpu as pltpu
from jax.sharding import PartitionSpec as P

LAYERS = 3
BLK = 32
RADIUS = 8
C = 32
SHIFTS = 2 * RADIUS + 1
HALO = RADIUS + LAYERS
RAW_ROWS = 64
GROUP = 6
LANES = 128
WIDTH = 256
WIN = 64
SPAN = WIN + 2 * RADIUS
JOINT = 4
STEPS = 5
DEEP = (BLK + JOINT) * C
BAND = 24
bf16 = jnp.bfloat16
f32 = jnp.float32


def pairs_even(n):
    return [(i, i ^ 1) for i in range(n) if (i ^ 1) < n]


def pairs_odd(n):
    return [(i, ((i + 1) ^ 1) - 1) for i in range(n) if 0 <= ((i + 1) ^ 1) - 1 < n]


def split(value):
    high = value.astype(bf16)
    return high, (value - high.astype(f32)).astype(bf16)


def dot(left, right):
    return jnp.dot(left, right, preferred_element_type=f32)


def iota(shape, axis):
    return lax.broadcasted_iota(jnp.int32, shape, axis)


def prepare(later_hbm, first_hbm, bias_hbm, image_hbm, t1, t2, t3, spread, image,
            later_ref, first_ref, bias_ref, arrived):
    copies = [
        pltpu.make_async_copy(source, target, arrived.at[i])
        for i, (source, target) in enumerate((
            (later_hbm, later_ref), (first_hbm, first_ref), (bias_hbm, bias_ref), (image_hbm, image)))
    ]
    for copy in copies:
        copy.start()
    for copy in copies:
        copy.wait()
    for layer, t in enumerate((t2, t3)):
        for kx in range(3):
            taps = [later_ref[layer, ky, kx] for ky in range(3)]
            wide = jnp.concatenate(taps + [jnp.zeros((C, LANES - 3 * C), f32)], axis=1)
            wide = jnp.concatenate([wide, jnp.zeros((C, LANES), f32)], axis=1)
            for yo in range(GROUP):
                high, low = split(pltpu.roll(wide, yo * C, 1) if yo else wide)
                rows = slice((yo * 3 + kx) * C, (yo * 3 + kx + 1) * C)
                t[0, rows, :] = high
                t[1, rows, :] = low
    offset = iota((16, WIDTH), 0) - iota((16, WIDTH), 1) // C
    pieces = []
    for kx in range(3):
        piece = jnp.zeros((16, WIDTH), f32)
        for ky in range(3):
            row = jnp.concatenate([first_ref[ky, kx]] * (WIDTH // C), axis=1)
            piece = jnp.where(offset == ky, jnp.broadcast_to(row, (16, WIDTH)), piece)
        pieces.append(piece)
    pieces.append(jnp.zeros((LANES - 48, WIDTH), f32))
    high, low = split(jnp.transpose(jnp.concatenate(pieces, 0)))
    t1[:, 0:48] = high[:, 0:48]
    t1[:, 48:96] = low[:, 0:48]
    t1[:, 96:144] = high[:, 0:48]
    b = jnp.concatenate([bias_ref[...], jnp.zeros((LAYERS, LANES - C), f32)], 1)
    b = jnp.transpose(jnp.concatenate([b, jnp.zeros((8 - LAYERS, LANES), f32)], 0))
    for layer in range(LAYERS):
        spread[layer] = jnp.broadcast_to(b[0:C, layer:layer + 1], (C, WIDTH))


def encode(image, base, groups, ends, tile, tiles, t1, t2, t3, spread, raw, x1, x2, emit):
    n1, n2 = 8 * groups[0], GROUP * groups[1]
    col = iota((RAW_ROWS, WIDTH), 1)
    raw[0] = jnp.where(col == 0, 0.0, pltpu.roll(image, 1, 1))
    raw[1] = image
    raw[2] = jnp.where(col == WIDTH - 1, 0.0, pltpu.roll(image, WIDTH - 1, 1))
    edge = iota((C, WIDTH), 1)

    def put(x, row, value):
        high, low = split(value)
        x[0, row * C:(row + 1) * C, :] = high
        x[1, row * C:(row + 1) * C, :] = low

    def outside(x, top, end, rows):
        @pl.when(tile == 0)
        def _():
            x[:, 0:top * C, :] = jnp.zeros((2, top * C, WIDTH), bf16)

        @pl.when(tile == tiles - 1)
        def _():
            x[:, end * C:rows * C, :] = jnp.zeros((2, (rows - end) * C, WIDTH), bf16)

    def conv(t, x, group, bias):
        rows = slice(group * GROUP * C, (group * GROUP + 8) * C)
        th, tl, xh, xl = t[0], t[1], x[0, rows, :], x[1, rows, :]
        r = dot(jnp.concatenate([th, tl, th], 1), jnp.concatenate([xh, xh, xl], 0))
        for yo in range(GROUP):
            a, b, c = (r[(yo * 3 + kx) * C:(yo * 3 + kx + 1) * C] for kx in range(3))
            a = jnp.where(edge == 0, 0.0, pltpu.roll(a, 1, 1))
            c = jnp.where(edge == WIDTH - 1, 0.0, pltpu.roll(c, WIDTH - 1, 1))
            yield group * GROUP + yo, a + b + c + bias

    for g in range(groups[0]):
        parts = [raw[kx, base + 8 * g:base + 8 * g + 16, :] for kx in range(3)]
        high, low = split(jnp.concatenate(parts, 0))
        r = dot(t1[...], jnp.concatenate([high, high, low], 0))
        for yo in range(8):
            put(x1, 8 * g + yo, jnp.tanh(r[yo * C:(yo + 1) * C] + spread[0]))
    outside(x1, ends[0], ends[1], n1)
    for g in range(groups[1]):
        for row, value in conv(t2, x1, g, spread[1]):
            put(x2, row, jnp.tanh(value))
    outside(x2, ends[2], ends[3], n2)
    for row in range(n2, GROUP * groups[2] + 2):
        x2[:, row * C:(row + 1) * C, :] = jnp.zeros((2, C, WIDTH), bf16)
    for g in range(groups[2]):
        for row, value in conv(t3, x2, g, spread[2]):
            emit(row, value)


def own_features(where, image_ref, t1, t2, t3, spread, packed, raw, x1, x2, kept):
    tile, tiles = where[0], where[1]
    pad = JOINT - 1
    kept[:, :, 0:pad * C, :] = jnp.zeros((2, 2, pad * C, WIDTH), bf16)
    kept[:, :, (pad + BLK) * C:, :] = jnp.zeros((2, 2, JOINT * C, WIDTH), bf16)

    def emit(row, value):
        if row >= BLK:
            return
        turned = [pltpu.roll(value[:, i:i + LANES], WIN, 1) for i in range(0, WIDTH, LANES)]
        rows = slice((row + pad) * C, (row + pad + 1) * C)
        for form, v in enumerate((value, jnp.concatenate(turned, 1))):
            kept[form, 0, rows, :], kept[form, 1, rows, :] = split(v)

    encode(image_ref[...], RADIUS, (5, 6, 6), (2, 34, 1, 33), tile, tiles,
           t1, t2, t3, spread, raw, x1, x2, emit)
    left = iota((C, LANES), 1) < WIN
    for w in range(WIDTH // WIN):
        half = slice((w // 2) * LANES, (w // 2 + 1) * LANES)
        for part in range(2):
            for y in range(BLK + JOINT):
                cols = []
                for g in (0, 2):
                    a = kept[w % 2, part, (y - g + pad) * C:(y - g + pad + 1) * C, half]
                    b = kept[1 - w % 2, part, (y - g - 1 + pad) * C:(y - g + pad) * C, half]
                    cols.append(jnp.where(left, a, b))
                packed[w, part, y * C:(y + 1) * C, :] = jnp.concatenate(cols, 1)


def correlate(where, pair, mask, own_ref, even_ref, odd_ref, t1, t2, t3, spread, packed, out_ref,
              raw, x1, x2, feats, turned):
    tile, tiles, section = where[0], where[1], where[2]
    image = jnp.where(pair[0] == section, own_ref[...],
                      jnp.where(pair[0] == (section ^ 1), even_ref[...], odd_ref[...]))

    def emit(row, value):
        feats[row * C:(row + 1) * C, :] = value

    encode(image, 0, (7, 9, 8), (10, 42, 9, 41), tile, tiles, t1, t2, t3, spread, raw, x1, x2, emit)

    @pl.when(tile == 0)
    def _():
        feats[0:RADIUS * C, :] = jnp.zeros((RADIUS * C, WIDTH), f32)

    @pl.when(tile == tiles - 1)
    def _():
        feats[(BLK + RADIUS) * C:, :] = jnp.zeros((RADIUS * C, WIDTH), f32)

    border = jnp.zeros((RADIUS, LANES), f32)
    turned[:, :, (BLK + 2 * RADIUS) * C:] = jnp.zeros((2, WIDTH + 2 * RADIUS, JOINT * C), bf16)
    for q in range((BLK + 2 * RADIUS) * C // LANES):
        cols = slice(q * LANES, (q + 1) * LANES)
        v = jnp.concatenate([border, jnp.transpose(feats[cols, :]), border], 0)
        turned[0, :, cols], turned[1, :, cols] = split(v)

    lane8, sub8 = iota((8, LANES), 1), iota((8, LANES), 0)
    eighth = (iota((8, WIDTH), 1) % WIN) // 8
    sums = [[None] * 8 for _ in range(JOINT)]
    for w in range(WIDTH // WIN):
        rows = slice(w * WIN, w * WIN + SPAN)
        lefts = []
        for j in range(STEPS):
            cols = slice(j * JOINT * C, j * JOINT * C + DEEP)
            high, low = turned[0, rows, cols], turned[1, rows, cols]
            lefts.append(jnp.concatenate([high, low, high], 1))
        right = jnp.concatenate([packed[w, 0], packed[w, 0], packed[w, 1]], 0)
        p = dot(jnp.concatenate(lefts, 0), right)
        bands = []
        for j in range(STEPS):
            for k in range(3):
                band = None
                for m in range(8):
                    start = j * SPAN + 8 * (m + k)
                    v = p[start:start + 8, :]
                    band = v if band is None else jnp.where(eighth == m, v, band)
                bands.append(band)
        bands.append(jnp.zeros((8, WIDTH), f32))
        flat = jnp.transpose(jnp.concatenate(bands, 0))
        for g in range(JOINT):
            for side in range(2):
                at = g * WIN + side * BLK
                v = flat[at:at + 8] + flat[at + 8:at + 16] + flat[at + 16:at + 24] + flat[at + 24:at + 32]
                for bit in (1, 2, 4):
                    v = jnp.where((sub8 & bit) != 0, pltpu.roll(v, LANES - bit, 1), v)
                sums[g][2 * w + side] = jnp.sum(v, axis=0, keepdims=True)
    total = jnp.zeros((8, 3 * LANES), f32)
    lane = iota((8, 3 * LANES), 1)
    for g in range(JOINT):
        d = jnp.concatenate(sums[g], 0)
        d = jnp.concatenate([d, jnp.zeros((8, 2 * LANES), f32)], 1)
        for j in range(STEPS):
            dy = JOINT * j + g
            if dy < SHIFTS:
                shift = (SHIFTS * dy - BAND * j) % (3 * LANES)
                here = (lane >= SHIFTS * dy) & (lane < SHIFTS * (dy + 1))
                total = jnp.where(here, pltpu.roll(d, shift, 1) if shift else d, total)
    weight = jnp.zeros((8, 3 * LANES), f32)
    for b in range(8):
        weight = jnp.where(iota((8, 3 * LANES), 0) == b, mask[b].astype(f32), weight)
    total = total * (weight * np.float32(1.0 / np.sqrt(BLK * BLK * C)))
    out_ref[...] = total[:, :SHIFTS * SHIFTS]


VMEM = pl.BlockSpec(memory_space=pltpu.VMEM)
HBM = pl.BlockSpec(memory_space=pltpu.HBM)
SMEM = pl.BlockSpec(memory_space=pltpu.SMEM)


def params(flops, moved, mib=40):
    return dict(
        compiler_params=pltpu.CompilerParams(vmem_limit_bytes=mib << 20),
        cost_estimate=pl.CostEstimate(flops=flops, bytes_accessed=moved, transcendentals=0),
    )


def scratch(rows1, rows2):
    return [
        pltpu.VMEM((3, RAW_ROWS, WIDTH), f32),
        pltpu.VMEM((2, rows1 * C, WIDTH), bf16),
        pltpu.VMEM((2, rows2 * C, WIDTH), bf16),
    ]


def body(raw_image, pairing, valid_mask, first_kernel, later_kernels, biases):
    tiles, sections = lax.axis_size("tile"), lax.axis_size("sec")
    tile, section = lax.axis_index("tile"), lax.axis_index("sec")
    image = raw_image[0]
    rows, width = image.shape
    shape = jax.ShapeDtypeStruct
    got_even = lax.ppermute(image, "tile", pairs_even(tiles))
    got_odd = lax.ppermute(image, "tile", pairs_odd(tiles))
    t1, t2, t3, spread, image = pl.pallas_call(
        prepare,
        out_shape=[shape((256, 144), bf16), shape((2, 576, 256), bf16), shape((2, 576, 256), bf16),
                   shape((LAYERS, C, WIDTH), f32), shape(image.shape, f32)],
        in_specs=[HBM] * 4, out_specs=[VMEM] * 5,
        scratch_shapes=[pltpu.VMEM((2, 3, 3, C, C), f32), pltpu.VMEM((3, 3, 1, C), f32),
                        pltpu.VMEM((LAYERS, C), f32), pltpu.SemaphoreType.DMA((4,))],
        name="prepare", **params(10**6, 3 * 10**6),
    )(*(pltpu.with_memory_space_constraint(v, pltpu.HBM) for v in (
        jnp.transpose(later_kernels, (0, 3, 4, 1, 2)), jnp.transpose(first_kernel, (2, 3, 1, 0)), biases, image)))

    odd_tile = (tile % 2) == 1
    above = jnp.where(odd_tile, got_even[rows - HALO:], got_odd[rows - HALO:])
    below = jnp.where(odd_tile, got_odd[:HALO], got_even[:HALO])
    own = jnp.concatenate([above, image, below, jnp.zeros((RAW_ROWS - rows - 2 * HALO, width), f32)], 0)
    even = lax.ppermute(own, "sec", pairs_even(sections))
    odd = lax.ppermute(own, "sec", pairs_odd(sections))
    where = jnp.stack([tile, jnp.int32(tiles), section]).astype(jnp.int32)
    packed = pl.pallas_call(
        own_features,
        out_shape=shape((WIDTH // WIN, 2, DEEP, WIDTH), bf16),
        in_specs=[SMEM] + [VMEM] * 5, out_specs=VMEM,
        scratch_shapes=scratch(40, 38) + [pltpu.VMEM((2, 2, (BLK + 2 * JOINT - 1) * C, WIDTH), bf16)],
        name="own_features", **params(5 * 10**9, 10**7),
    )(where, own, t1, t2, t3, spread)
    result = pl.pallas_call(
        correlate,
        out_shape=shape((8, SHIFTS * SHIFTS), f32),
        in_specs=[SMEM] * 3 + [VMEM] * 8, out_specs=VMEM,
        scratch_shapes=scratch(56, 54) + [
            pltpu.VMEM(((BLK + 2 * RADIUS) * C, WIDTH), f32),
            pltpu.VMEM((2, WIDTH + 2 * RADIUS, (BLK + 2 * RADIUS + JOINT) * C), bf16),
        ],
        name="correlate", **params(10**10, 10**7),
    )(where, pairing, valid_mask.reshape(-1), own, even, odd, t1, t2, t3, spread, packed)
    return result[None, None]


def solution(mesh):
    placed = (
        P(("groups", "sec"), "tile", None),
        P(("groups", "sec")),
        P(("groups", "sec"), "tile", None),
        P(),
        P(),
        P(),
    )
    return jax.shard_map(
        body,
        mesh=mesh,
        in_specs=placed,
        out_specs=P(("groups", "sec"), "tile", None, None),
        check_vma=False,
    )
```

```python
import jax
import jax.numpy as jnp
import numpy as np
from jax import lax
from jax.experimental import pallas as pl
from jax.experimental.pallas import tpu as pltpu
from jax.sharding import PartitionSpec as P

LAYERS = 3
BLK = 32
RADIUS = 8
C = 32
SHIFTS = 2 * RADIUS + 1
HALO = RADIUS + LAYERS
RAW_ROWS = 64
LANES = 128
WIDTH = 256
WIN = 64
SPAN = WIN + 2 * RADIUS
JOINT = 4
STEPS = 5
DEEP = (BLK + JOINT) * C
BAND = 24
STREAMS = ((1, 2), (None, 0), (0, 1), (2, None))
FORMS = ((1, 0), (2, 1), (0, None), (None, 2))
bf16 = jnp.bfloat16
f32 = jnp.float32


def pairs_even(n):
    return [(i, i ^ 1) for i in range(n) if (i ^ 1) < n]


def pairs_odd(n):
    return [(i, ((i + 1) ^ 1) - 1) for i in range(n) if 0 <= ((i + 1) ^ 1) - 1 < n]


def split(value):
    high = value.astype(bf16)
    return high, (value - high.astype(f32)).astype(bf16)


def dot(left, right):
    return jnp.dot(left, right, preferred_element_type=f32)


def iota(shape, axis):
    return lax.broadcasted_iota(jnp.int32, shape, axis)


def prepare(later_hbm, first_hbm, bias_hbm, image_hbm, t1, t2, t3, spread, order, image,
            later_ref, first_ref, bias_ref, arrived):
    copies = [
        pltpu.make_async_copy(source, target, arrived.at[i])
        for i, (source, target) in enumerate((
            (later_hbm, later_ref), (first_hbm, first_ref), (bias_hbm, bias_ref), (image_hbm, image)))
    ]
    for copy in copies:
        copy.start()
    row, col = iota((WIDTH, WIDTH), 0), iota((WIDTH, WIDTH), 1)
    order[0:WIDTH, :] = jnp.where(row == 2 * (col % LANES) + col // LANES, 1.0, 0.0).astype(bf16)
    order[WIDTH:, :] = jnp.where(col == 2 * (row % LANES) + row // LANES, 1.0, 0.0).astype(bf16)
    for copy in copies:
        copy.wait()
    nothing = jnp.zeros((C, C), f32)
    for layer, t in enumerate((t2, t3)):
        for stream, (even, odd) in enumerate(STREAMS):
            taps = []
            for ky in range(3):
                taps += [nothing if kx is None else later_ref[layer, ky, kx] for kx in (even, odd)]
            wide = jnp.concatenate(taps + [nothing, nothing], axis=1)
            for yo in range(2):
                high, low = split(pltpu.roll(wide, yo * 2 * C, 1) if yo else wide)
                rows = slice((yo * 4 + stream) * C, (yo * 4 + stream + 1) * C)
                t[0, rows, :] = high
                t[1, rows, :] = low
    shape = (16, 8 * 2 * C)
    offset = iota(shape, 0) - iota(shape, 1) // (2 * C)
    pieces = []
    for even, odd in FORMS:
        piece = jnp.zeros(shape, f32)
        for ky in range(3):
            pair = [jnp.zeros((1, C), f32) if kx is None else first_ref[ky, kx] for kx in (even, odd)]
            piece = jnp.where(offset == ky, jnp.broadcast_to(jnp.concatenate(pair * 8, 1), shape), piece)
        pieces.append(piece)
    pieces.append(jnp.zeros((64, 8 * 2 * C), f32))
    high, low = split(jnp.transpose(jnp.concatenate(pieces, 0)))
    t1[:, 0:64] = high[:, 0:64]
    t1[:, 64:128] = low[:, 0:64]
    t1[:, 128:192] = high[:, 0:64]
    b = jnp.concatenate([bias_ref[...], jnp.zeros((LAYERS, LANES - C), f32)], 1)
    b = jnp.transpose(jnp.concatenate([b, jnp.zeros((8 - LAYERS, LANES), f32)], 0))
    for layer in range(LAYERS):
        spread[layer] = jnp.broadcast_to(b[0:C, layer:layer + 1], (C, WIDTH))


def encode(image, starts, groups, ends, tile, tiles, t1, t2, t3, spread, order, raw, x1, x2, x3, emit):
    n1, n2, n3 = 8 * groups[0], 2 * groups[1], 2 * groups[2]
    h = image.astype(bf16)
    rest = image - h.astype(f32)
    m = rest.astype(bf16)
    l = (rest - m.astype(f32)).astype(bf16)
    apart = order[0:WIDTH, :]
    image = dot(jnp.concatenate([h, m, l], 1), jnp.concatenate([apart] * 3, 0))
    even, odd = image[:, :LANES], image[:, LANES:]
    col = iota((RAW_ROWS, LANES), 1)
    before = jnp.where(col == 0, 0.0, pltpu.roll(odd, 1, 1))
    after = jnp.where(col == LANES - 1, 0.0, pltpu.roll(even, LANES - 1, 1))
    for form, v in enumerate((even, odd, before, after)):
        raw[form] = jnp.concatenate([v[a:a + n1 + 8] for a in starts], 1)
    lane = iota((C, WIDTH), 1) % LANES
    twice = lambda v: jnp.concatenate([v, v], 0)

    def put(x, row, value):
        high, low = split(value)
        x[0, row * 2 * C:(row + 1) * 2 * C, :] = high
        x[1, row * 2 * C:(row + 1) * 2 * C, :] = low

    def outside(x, top, end, rows):
        @pl.when(tile == 0)
        def _():
            x[:, 0:top * 2 * C, 0:LANES] = jnp.zeros((2, top * 2 * C, LANES), bf16)

        @pl.when(tile == tiles - 1)
        def _():
            x[:, end * 2 * C:rows * 2 * C, LANES:] = jnp.zeros((2, (rows - end) * 2 * C, LANES), bf16)

    def shifted(v, by, blank):
        v = jnp.concatenate([pltpu.roll(v[:, i:i + LANES], by, 1) for i in range(0, WIDTH, LANES)], 1)
        return jnp.where(lane == blank, 0.0, v)

    def conv(t, x, step, bias):
        rows = slice(step * 4 * C, (step * 4 + 8) * C)
        th, tl, xh, xl = t[0], t[1], x[0, rows, :], x[1, rows, :]
        r = dot(jnp.concatenate([th, tl, th], 1), jnp.concatenate([xh, xh, xl], 0))
        for yo in range(2):
            a, b, c, d = (r[(yo * 4 + i) * C:(yo * 4 + i + 1) * C] for i in range(4))
            yield 2 * step + yo, a + shifted(b, 1, 0) + bias, c + shifted(d, LANES - 1, LANES - 1) + bias

    for g in range(groups[0]):
        high, low = split(jnp.concatenate([raw[form, 8 * g:8 * g + 16, :] for form in range(4)], 0))
        r = dot(t1[...], jnp.concatenate([high, high, low], 0))
        for yo in range(8):
            put(x1, 8 * g + yo, jnp.tanh(r[yo * 2 * C:(yo + 1) * 2 * C] + twice(spread[0])))
    outside(x1, ends[0], ends[1], n1)
    for step in range(groups[1]):
        for row, a, b in conv(t2, x1, step, spread[1]):
            put(x2, row, jnp.tanh(jnp.concatenate([a, b], 0)))
    outside(x2, ends[2], ends[3], n2)
    for step in range(groups[2]):
        for row, a, b in conv(t3, x2, step, spread[2]):
            for run in range(2):
                rows = slice((run * n3 + row) * C, (run * n3 + row + 1) * C)
                for parity, v in enumerate((a, b)):
                    high, low = split(v[:, run * LANES:(run + 1) * LANES])
                    x3[rows, parity * LANES:(parity + 1) * LANES] = high
                    x3[rows, WIDTH + parity * LANES:WIDTH + (parity + 1) * LANES] = low
    together = jnp.concatenate([order[WIDTH:, :]] * 2, 0)
    for row in range(0, 2 * n3, 16):
        r = dot(x3[row * C:(row + 16) * C, :], together)
        for i in range(16):
            emit(row + i, r[i * C:(i + 1) * C])


def own_features(where, image_ref, t1, t2, t3, spread, order, packed, raw, x1, x2, x3, kept):
    tile, tiles = where[0], where[1]
    pad = JOINT - 1
    kept[:, :, 0:pad * C, :] = jnp.zeros((2, 2, pad * C, WIDTH), bf16)
    kept[:, :, (pad + BLK) * C:, :] = jnp.zeros((2, 2, JOINT * C, WIDTH), bf16)

    def emit(row, value):
        turned = [pltpu.roll(value[:, i:i + LANES], WIN, 1) for i in range(0, WIDTH, LANES)]
        rows = slice((row + pad) * C, (row + pad + 1) * C)
        for form, v in enumerate((value, jnp.concatenate(turned, 1))):
            kept[form, 0, rows, :], kept[form, 1, rows, :] = split(v)

    encode(image_ref[...], (8, 24), (3, 9, 8), (2, 18, 1, 17), tile, tiles,
           t1, t2, t3, spread, order, raw, x1, x2, x3, emit)
    left = iota((C, LANES), 1) < WIN
    for w in range(WIDTH // WIN):
        half = slice((w // 2) * LANES, (w // 2 + 1) * LANES)
        for part in range(2):
            for y in range(BLK + JOINT):
                cols = []
                for g in (0, 2):
                    a = kept[w % 2, part, (y - g + pad) * C:(y - g + pad + 1) * C, half]
                    b = kept[1 - w % 2, part, (y - g - 1 + pad) * C:(y - g + pad) * C, half]
                    cols.append(jnp.where(left, a, b))
                packed[w, part, y * C:(y + 1) * C, :] = jnp.concatenate(cols, 1)


def correlate(where, pair, mask, own_ref, even_ref, odd_ref, t1, t2, t3, spread, order, packed, out_ref,
              raw, x1, x2, x3, feats, turned):
    tile, tiles, section = where[0], where[1], where[2]
    image = jnp.where(pair[0] == section, own_ref[...],
                      jnp.where(pair[0] == (section ^ 1), even_ref[...], odd_ref[...]))

    def emit(row, value):
        feats[row * C:(row + 1) * C, :] = value

    encode(image, (0, 24), (4, 13, 12), (10, 18, 9, 17), tile, tiles,
           t1, t2, t3, spread, order, raw, x1, x2, x3, emit)

    @pl.when(tile == 0)
    def _():
        feats[0:RADIUS * C, :] = jnp.zeros((RADIUS * C, WIDTH), f32)

    @pl.when(tile == tiles - 1)
    def _():
        feats[(BLK + RADIUS) * C:, :] = jnp.zeros((RADIUS * C, WIDTH), f32)

    border = jnp.zeros((RADIUS, LANES), f32)
    turned[:, :, (BLK + 2 * RADIUS) * C:] = jnp.zeros((2, WIDTH + 2 * RADIUS, JOINT * C), bf16)
    for q in range((BLK + 2 * RADIUS) * C // LANES):
        cols = slice(q * LANES, (q + 1) * LANES)
        v = jnp.concatenate([border, jnp.transpose(feats[cols, :]), border], 0)
        turned[0, :, cols], turned[1, :, cols] = split(v)

    lane8, sub8 = iota((8, LANES), 1), iota((8, LANES), 0)
    eighth = (iota((8, WIDTH), 1) % WIN) // 8
    sums = [[None] * 8 for _ in range(JOINT)]
    for w in range(WIDTH // WIN):
        rows = slice(w * WIN, w * WIN + SPAN)
        lefts = []
        for j in range(STEPS):
            cols = slice(j * JOINT * C, j * JOINT * C + DEEP)
            high, low = turned[0, rows, cols], turned[1, rows, cols]
            lefts.append(jnp.concatenate([high, low, high], 1))
        right = jnp.concatenate([packed[w, 0], packed[w, 0], packed[w, 1]], 0)
        p = dot(jnp.concatenate(lefts, 0), right)
        bands = []
        for j in range(STEPS):
            for k in range(3):
                band = None
                for m in range(8):
                    start = j * SPAN + 8 * (m + k)
                    v = p[start:start + 8, :]
                    band = v if band is None else jnp.where(eighth == m, v, band)
                bands.append(band)
        bands.append(jnp.zeros((8, WIDTH), f32))
        flat = jnp.transpose(jnp.concatenate(bands, 0))
        for g in range(JOINT):
            for side in range(2):
                at = g * WIN + side * BLK
                v = flat[at:at + 8] + flat[at + 8:at + 16] + flat[at + 16:at + 24] + flat[at + 24:at + 32]
                for bit in (1, 2, 4):
                    v = jnp.where((sub8 & bit) != 0, pltpu.roll(v, LANES - bit, 1), v)
                sums[g][2 * w + side] = jnp.sum(v, axis=0, keepdims=True)
    total = jnp.zeros((8, 3 * LANES), f32)
    lane = iota((8, 3 * LANES), 1)
    for g in range(JOINT):
        d = jnp.concatenate(sums[g], 0)
        d = jnp.concatenate([d, jnp.zeros((8, 2 * LANES), f32)], 1)
        for j in range(STEPS):
            dy = JOINT * j + g
            if dy < SHIFTS:
                shift = (SHIFTS * dy - BAND * j) % (3 * LANES)
                here = (lane >= SHIFTS * dy) & (lane < SHIFTS * (dy + 1))
                total = jnp.where(here, pltpu.roll(d, shift, 1) if shift else d, total)
    weight = jnp.zeros((8, 3 * LANES), f32)
    for b in range(8):
        weight = jnp.where(iota((8, 3 * LANES), 0) == b, mask[b].astype(f32), weight)
    total = total * (weight * np.float32(1.0 / np.sqrt(BLK * BLK * C)))
    out_ref[...] = total[:, :SHIFTS * SHIFTS]


VMEM = pl.BlockSpec(memory_space=pltpu.VMEM)
HBM = pl.BlockSpec(memory_space=pltpu.HBM)
SMEM = pl.BlockSpec(memory_space=pltpu.SMEM)


def params(flops, moved, mib=40):
    return dict(
        compiler_params=pltpu.CompilerParams(vmem_limit_bytes=mib << 20),
        cost_estimate=pl.CostEstimate(flops=flops, bytes_accessed=moved, transcendentals=0),
    )


def scratch(rows1, rows2, rows3):
    return [
        pltpu.VMEM((4, rows1 + 8, WIDTH), f32),
        pltpu.VMEM((2, rows1 * 2 * C, WIDTH), bf16),
        pltpu.VMEM((2, rows2 * 2 * C, WIDTH), bf16),
        pltpu.VMEM((rows3 * C, 2 * WIDTH), bf16),
    ]


def body(raw_image, pairing, valid_mask, first_kernel, later_kernels, biases):
    tiles, sections = lax.axis_size("tile"), lax.axis_size("sec")
    tile, section = lax.axis_index("tile"), lax.axis_index("sec")
    image = raw_image[0]
    rows, width = image.shape
    shape = jax.ShapeDtypeStruct
    got_even = lax.ppermute(image, "tile", pairs_even(tiles))
    got_odd = lax.ppermute(image, "tile", pairs_odd(tiles))
    t1, t2, t3, spread, order, image = pl.pallas_call(
        prepare,
        out_shape=[shape((512, 192), bf16), shape((2, WIDTH, WIDTH), bf16), shape((2, WIDTH, WIDTH), bf16),
                   shape((LAYERS, C, WIDTH), f32), shape((2 * WIDTH, WIDTH), bf16), shape(image.shape, f32)],
        in_specs=[HBM] * 4, out_specs=[VMEM] * 6,
        scratch_shapes=[pltpu.VMEM((2, 3, 3, C, C), f32), pltpu.VMEM((3, 3, 1, C), f32),
                        pltpu.VMEM((LAYERS, C), f32), pltpu.SemaphoreType.DMA((4,))],
        name="prepare", **params(10**6, 3 * 10**6),
    )(*(pltpu.with_memory_space_constraint(v, pltpu.HBM) for v in (
        jnp.transpose(later_kernels, (0, 3, 4, 1, 2)), jnp.transpose(first_kernel, (2, 3, 1, 0)), biases, image)))

    odd_tile = (tile % 2) == 1
    above = jnp.where(odd_tile, got_even[rows - HALO:], got_odd[rows - HALO:])
    below = jnp.where(odd_tile, got_odd[:HALO], got_even[:HALO])
    own = jnp.concatenate([above, image, below, jnp.zeros((RAW_ROWS - rows - 2 * HALO, width), f32)], 0)
    even = lax.ppermute(own, "sec", pairs_even(sections))
    odd = lax.ppermute(own, "sec", pairs_odd(sections))
    where = jnp.stack([tile, jnp.int32(tiles), section]).astype(jnp.int32)
    packed = pl.pallas_call(
        own_features,
        out_shape=shape((WIDTH // WIN, 2, DEEP, WIDTH), bf16),
        in_specs=[SMEM] + [VMEM] * 6, out_specs=VMEM,
        scratch_shapes=scratch(24, 18, 32) + [pltpu.VMEM((2, 2, (BLK + 2 * JOINT - 1) * C, WIDTH), bf16)],
        name="own_features", **params(5 * 10**9, 10**7),
    )(where, own, t1, t2, t3, spread, order)
    result = pl.pallas_call(
        correlate,
        out_shape=shape((8, SHIFTS * SHIFTS), f32),
        in_specs=[SMEM] * 3 + [VMEM] * 9, out_specs=VMEM,
        scratch_shapes=scratch(32, 26, 48) + [
            pltpu.VMEM(((BLK + 2 * RADIUS) * C, WIDTH), f32),
            pltpu.VMEM((2, WIDTH + 2 * RADIUS, (BLK + 2 * RADIUS + JOINT) * C), bf16),
        ],
        name="correlate", **params(10**10, 10**7),
    )(where, pairing, valid_mask.reshape(-1), own, even, odd, t1, t2, t3, spread, order, packed)
    return result[None, None]


def solution(mesh):
    placed = (
        P(("groups", "sec"), "tile", None),
        P(("groups", "sec")),
        P(("groups", "sec"), "tile", None),
        P(),
        P(),
        P(),
    )
    return jax.shard_map(
        body,
        mesh=mesh,
        in_specs=placed,
        out_specs=P(("groups", "sec"), "tile", None, None),
        check_vma=False,
    )
```

```python
import jax
import jax.numpy as jnp
import numpy as np
from jax import lax
from jax.experimental import pallas as pl
from jax.experimental.pallas import tpu as pltpu
from jax.sharding import PartitionSpec as P

LAYERS = 3
BLK = 32
RADIUS = 8
C = 32
SHIFTS = 2 * RADIUS + 1
HALO = RADIUS + LAYERS
RAW_ROWS = 64
LANES = 128
WIDTH = 256
WIN = 64
SPAN = WIN + 2 * RADIUS
JOINT = 4
STEPS = 5
DEEP = (BLK + JOINT) * C
BAND = 24
STREAMS = ((1, 2), (None, 0), (0, 1), (2, None))
FORMS = ((1, 0), (2, 1), (0, None), (None, 2))
bf16 = jnp.bfloat16
f32 = jnp.float32


def pairs_even(n):
    return [(i, i ^ 1) for i in range(n) if (i ^ 1) < n]


def pairs_odd(n):
    return [(i, ((i + 1) ^ 1) - 1) for i in range(n) if 0 <= ((i + 1) ^ 1) - 1 < n]


def split(value):
    high = value.astype(bf16)
    return high, (value - high.astype(f32)).astype(bf16)


def dot(left, right):
    return jnp.dot(left, right, preferred_element_type=f32)


def iota(shape, axis):
    return lax.broadcasted_iota(jnp.int32, shape, axis)


def prepare(later_hbm, first_hbm, bias_hbm, image_hbm, mask_hbm, pair_ref,
            t1, t2, t3, spread, order, image, scale, choice,
            later_ref, first_ref, bias_ref, mask_ref, arrived):
    copies = [
        pltpu.make_async_copy(source, target, arrived.at[i])
        for i, (source, target) in enumerate((
            (later_hbm, later_ref), (first_hbm, first_ref), (bias_hbm, bias_ref), (image_hbm, image),
            (mask_hbm, mask_ref)))
    ]
    for copy in copies:
        copy.start()
    row, col = iota((WIDTH, WIDTH), 0), iota((WIDTH, WIDTH), 1)
    order[0:WIDTH, :] = jnp.where(row == 2 * (col % LANES) + col // LANES, 1.0, 0.0).astype(bf16)
    order[WIDTH:, :] = jnp.where(col == 2 * (row % LANES) + row // LANES, 1.0, 0.0).astype(bf16)
    for copy in copies:
        copy.wait()
    section, pair = lax.axis_index("sec"), pair_ref[0]
    which = jnp.where(pair == section, 0, jnp.where(pair == (section ^ 1), 1, 2))
    choice[...] = jnp.broadcast_to(which, choice.shape)
    mask = jnp.concatenate([mask_ref[...].astype(f32), jnp.zeros((1, LANES - 8), f32)], 1)
    mask = jnp.transpose(jnp.broadcast_to(mask, (8, LANES)))[0:8, 0:1]
    scale[...] = jnp.broadcast_to(mask * np.float32(1.0 / np.sqrt(BLK * BLK * C)), scale.shape)
    nothing = jnp.zeros((C, C), f32)
    for layer, t in enumerate((t2, t3)):
        for stream, (even, odd) in enumerate(STREAMS):
            taps = []
            for ky in range(3):
                taps += [nothing if kx is None else later_ref[layer, ky, kx] for kx in (even, odd)]
            wide = jnp.concatenate(taps + [nothing, nothing], axis=1)
            for yo in range(2):
                high, low = split(pltpu.roll(wide, yo * 2 * C, 1) if yo else wide)
                rows = slice((yo * 4 + stream) * C, (yo * 4 + stream + 1) * C)
                t[0, rows, :] = high
                t[1, rows, :] = low
    shape = (16, 8 * 2 * C)
    offset = iota(shape, 0) - iota(shape, 1) // (2 * C)
    pieces = []
    for even, odd in FORMS:
        piece = jnp.zeros(shape, f32)
        for ky in range(3):
            pair = [jnp.zeros((1, C), f32) if kx is None else first_ref[ky, kx] for kx in (even, odd)]
            piece = jnp.where(offset == ky, jnp.broadcast_to(jnp.concatenate(pair * 8, 1), shape), piece)
        pieces.append(piece)
    pieces.append(jnp.zeros((64, 8 * 2 * C), f32))
    high, low = split(jnp.transpose(jnp.concatenate(pieces, 0)))
    t1[:, 0:64] = high[:, 0:64]
    t1[:, 64:128] = low[:, 0:64]
    t1[:, 128:192] = high[:, 0:64]
    b = jnp.concatenate([bias_ref[...], jnp.zeros((LAYERS, LANES - C), f32)], 1)
    b = jnp.transpose(jnp.concatenate([b, jnp.zeros((8 - LAYERS, LANES), f32)], 0))
    for layer in range(LAYERS):
        spread[layer] = jnp.broadcast_to(b[0:C, layer:layer + 1], (C, WIDTH))


def encode(image, starts, groups, ends, tile, tiles, t1, t2, t3, spread, order, raw, x1, x2, x3, emit):
    n1, n2, n3 = 8 * groups[0], 2 * groups[1], 2 * groups[2]
    h = image.astype(bf16)
    rest = image - h.astype(f32)
    m = rest.astype(bf16)
    l = (rest - m.astype(f32)).astype(bf16)
    apart = order[0:WIDTH, :]
    image = dot(jnp.concatenate([h, m, l], 1), jnp.concatenate([apart] * 3, 0))
    even, odd = image[:, :LANES], image[:, LANES:]
    col = iota((RAW_ROWS, LANES), 1)
    before = jnp.where(col == 0, 0.0, pltpu.roll(odd, 1, 1))
    after = jnp.where(col == LANES - 1, 0.0, pltpu.roll(even, LANES - 1, 1))
    for form, v in enumerate((even, odd, before, after)):
        raw[form] = jnp.concatenate([v[a:a + n1 + 8] for a in starts], 1)
    lane = iota((C, WIDTH), 1) % LANES
    twice = lambda v: jnp.concatenate([v, v], 0)

    def put(x, row, value):
        high, low = split(value)
        x[0, row * 2 * C:(row + 1) * 2 * C, :] = high
        x[1, row * 2 * C:(row + 1) * 2 * C, :] = low

    def outside(x, top, end, rows):
        @pl.when(tile == 0)
        def _():
            x[:, 0:top * 2 * C, 0:LANES] = jnp.zeros((2, top * 2 * C, LANES), bf16)

        @pl.when(tile == tiles - 1)
        def _():
            x[:, end * 2 * C:rows * 2 * C, LANES:] = jnp.zeros((2, (rows - end) * 2 * C, LANES), bf16)

    def shifted(v, by, blank):
        v = jnp.concatenate([pltpu.roll(v[:, i:i + LANES], by, 1) for i in range(0, WIDTH, LANES)], 1)
        return jnp.where(lane == blank, 0.0, v)

    def conv(t, x, step, bias):
        rows = slice(step * 4 * C, (step * 4 + 8) * C)
        th, tl, xh, xl = t[0], t[1], x[0, rows, :], x[1, rows, :]
        r = dot(jnp.concatenate([th, tl, th], 1), jnp.concatenate([xh, xh, xl], 0))
        for yo in range(2):
            a, b, c, d = (r[(yo * 4 + i) * C:(yo * 4 + i + 1) * C] for i in range(4))
            yield 2 * step + yo, a + shifted(b, 1, 0) + bias, c + shifted(d, LANES - 1, LANES - 1) + bias

    for g in range(groups[0]):
        high, low = split(jnp.concatenate([raw[form, 8 * g:8 * g + 16, :] for form in range(4)], 0))
        r = dot(t1[...], jnp.concatenate([high, high, low], 0))
        for yo in range(8):
            put(x1, 8 * g + yo, jnp.tanh(r[yo * 2 * C:(yo + 1) * 2 * C] + twice(spread[0])))
    outside(x1, ends[0], ends[1], n1)
    for step in range(groups[1]):
        for row, a, b in conv(t2, x1, step, spread[1]):
            put(x2, row, jnp.tanh(jnp.concatenate([a, b], 0)))
    outside(x2, ends[2], ends[3], n2)
    for step in range(groups[2]):
        for row, a, b in conv(t3, x2, step, spread[2]):
            for run in range(2):
                rows = slice((run * n3 + row) * C, (run * n3 + row + 1) * C)
                for parity, v in enumerate((a, b)):
                    high, low = split(v[:, run * LANES:(run + 1) * LANES])
                    x3[rows, parity * LANES:(parity + 1) * LANES] = high
                    x3[rows, WIDTH + parity * LANES:WIDTH + (parity + 1) * LANES] = low
    together = jnp.concatenate([order[WIDTH:, :]] * 2, 0)
    for row in range(0, 2 * n3, 16):
        r = dot(x3[row * C:(row + 16) * C, :], together)
        for i in range(16):
            emit(row + i, r[i * C:(i + 1) * C])


def own_features(image_ref, t1, t2, t3, spread, order, packed, raw, x1, x2, x3, kept):
    tile, tiles = lax.axis_index("tile"), lax.axis_size("tile")
    pad = JOINT - 1
    kept[:, :, 0:pad * C, :] = jnp.zeros((2, 2, pad * C, WIDTH), bf16)
    kept[:, :, (pad + BLK) * C:, :] = jnp.zeros((2, 2, JOINT * C, WIDTH), bf16)

    def emit(row, value):
        turned = [pltpu.roll(value[:, i:i + LANES], WIN, 1) for i in range(0, WIDTH, LANES)]
        rows = slice((row + pad) * C, (row + pad + 1) * C)
        for form, v in enumerate((value, jnp.concatenate(turned, 1))):
            kept[form, 0, rows, :], kept[form, 1, rows, :] = split(v)

    encode(image_ref[...], (8, 24), (3, 9, 8), (2, 18, 1, 17), tile, tiles,
           t1, t2, t3, spread, order, raw, x1, x2, x3, emit)
    left = iota((C, LANES), 1) < WIN
    for w in range(WIDTH // WIN):
        half = slice((w // 2) * LANES, (w // 2 + 1) * LANES)
        for part in range(2):
            for y in range(BLK + JOINT):
                cols = []
                for g in (0, 2):
                    a = kept[w % 2, part, (y - g + pad) * C:(y - g + pad + 1) * C, half]
                    b = kept[1 - w % 2, part, (y - g - 1 + pad) * C:(y - g + pad) * C, half]
                    cols.append(jnp.where(left, a, b))
                packed[w, part, y * C:(y + 1) * C, :] = jnp.concatenate(cols, 1)


def correlate(choice, scale, own_ref, even_ref, odd_ref, t1, t2, t3, spread, order, packed, out_ref,
              raw, x1, x2, x3, feats, turned):
    tile, tiles = lax.axis_index("tile"), lax.axis_size("tile")
    which = choice[...]
    image = jnp.where(which == 0, own_ref[...], jnp.where(which == 1, even_ref[...], odd_ref[...]))

    def emit(row, value):
        feats[row * C:(row + 1) * C, :] = value

    encode(image, (0, 24), (4, 13, 12), (10, 18, 9, 17), tile, tiles,
           t1, t2, t3, spread, order, raw, x1, x2, x3, emit)

    @pl.when(tile == 0)
    def _():
        feats[0:RADIUS * C, :] = jnp.zeros((RADIUS * C, WIDTH), f32)

    @pl.when(tile == tiles - 1)
    def _():
        feats[(BLK + RADIUS) * C:, :] = jnp.zeros((RADIUS * C, WIDTH), f32)

    border = jnp.zeros((RADIUS, LANES), f32)
    turned[:, :, (BLK + 2 * RADIUS) * C:] = jnp.zeros((2, WIDTH + 2 * RADIUS, JOINT * C), bf16)
    for q in range((BLK + 2 * RADIUS) * C // LANES):
        cols = slice(q * LANES, (q + 1) * LANES)
        v = jnp.concatenate([border, jnp.transpose(feats[cols, :]), border], 0)
        turned[0, :, cols], turned[1, :, cols] = split(v)

    lane8, sub8 = iota((8, LANES), 1), iota((8, LANES), 0)
    eighth = (iota((8, WIDTH), 1) % WIN) // 8
    sums = [[None] * 8 for _ in range(JOINT)]
    for w in range(WIDTH // WIN):
        rows = slice(w * WIN, w * WIN + SPAN)
        lefts = []
        for j in range(STEPS):
            cols = slice(j * JOINT * C, j * JOINT * C + DEEP)
            high, low = turned[0, rows, cols], turned[1, rows, cols]
            lefts.append(jnp.concatenate([high, low, high], 1))
        right = jnp.concatenate([packed[w, 0], packed[w, 0], packed[w, 1]], 0)
        p = dot(jnp.concatenate(lefts, 0), right)
        bands = []
        for j in range(STEPS):
            for k in range(3):
                band = None
                for m in range(8):
                    start = j * SPAN + 8 * (m + k)
                    v = p[start:start + 8, :]
                    band = v if band is None else jnp.where(eighth == m, v, band)
                bands.append(band)
        bands.append(jnp.zeros((8, WIDTH), f32))
        flat = jnp.transpose(jnp.concatenate(bands, 0))
        for g in range(JOINT):
            for side in range(2):
                at = g * WIN + side * BLK
                v = flat[at:at + 8] + flat[at + 8:at + 16] + flat[at + 16:at + 24] + flat[at + 24:at + 32]
                for bit in (1, 2, 4):
                    v = jnp.where((sub8 & bit) != 0, pltpu.roll(v, LANES - bit, 1), v)
                sums[g][2 * w + side] = jnp.sum(v, axis=0, keepdims=True)
    total = jnp.zeros((8, 3 * LANES), f32)
    lane = iota((8, 3 * LANES), 1)
    for g in range(JOINT):
        d = jnp.concatenate(sums[g], 0)
        d = jnp.concatenate([d, jnp.zeros((8, 2 * LANES), f32)], 1)
        for j in range(STEPS):
            dy = JOINT * j + g
            if dy < SHIFTS:
                shift = (SHIFTS * dy - BAND * j) % (3 * LANES)
                here = (lane >= SHIFTS * dy) & (lane < SHIFTS * (dy + 1))
                total = jnp.where(here, pltpu.roll(d, shift, 1) if shift else d, total)
    total = total * scale[...]
    out_ref[...] = total[:, :SHIFTS * SHIFTS]


VMEM = pl.BlockSpec(memory_space=pltpu.VMEM)
HBM = pl.BlockSpec(memory_space=pltpu.HBM)


def params(flops, moved, mib=40):
    return dict(
        compiler_params=pltpu.CompilerParams(vmem_limit_bytes=mib << 20),
        cost_estimate=pl.CostEstimate(flops=flops, bytes_accessed=moved, transcendentals=0),
    )


def scratch(rows1, rows2, rows3):
    return [
        pltpu.VMEM((4, rows1 + 8, WIDTH), f32),
        pltpu.VMEM((2, rows1 * 2 * C, WIDTH), bf16),
        pltpu.VMEM((2, rows2 * 2 * C, WIDTH), bf16),
        pltpu.VMEM((rows3 * C, 2 * WIDTH), bf16),
    ]


def body(raw_image, pairing, valid_mask, first_kernel, later_kernels, biases):
    tiles, sections = lax.axis_size("tile"), lax.axis_size("sec")
    tile = lax.axis_index("tile")
    image = raw_image[0]
    rows, width = image.shape
    shape = jax.ShapeDtypeStruct
    got_even = lax.ppermute(image, "tile", pairs_even(tiles))
    got_odd = lax.ppermute(image, "tile", pairs_odd(tiles))
    t1, t2, t3, spread, order, image, scale, choice = pl.pallas_call(
        prepare,
        out_shape=[shape((512, 192), bf16), shape((2, WIDTH, WIDTH), bf16), shape((2, WIDTH, WIDTH), bf16),
                   shape((LAYERS, C, WIDTH), f32), shape((2 * WIDTH, WIDTH), bf16), shape(image.shape, f32), shape((8, 3 * LANES), f32),
                   shape((RAW_ROWS, WIDTH), jnp.int32)],
        in_specs=[HBM] * 5 + [pl.BlockSpec(memory_space=pltpu.SMEM)], out_specs=[VMEM] * 8,
        scratch_shapes=[pltpu.VMEM((2, 3, 3, C, C), f32), pltpu.VMEM((3, 3, 1, C), f32),
                        pltpu.VMEM((LAYERS, C), f32), pltpu.VMEM((1, 8), jnp.int32),
                        pltpu.SemaphoreType.DMA((5,))],
        name="prepare", **params(10**6, 3 * 10**6),
    )(*(pltpu.with_memory_space_constraint(v, pltpu.HBM) for v in (
        jnp.transpose(later_kernels, (0, 3, 4, 1, 2)), jnp.transpose(first_kernel, (2, 3, 1, 0)), biases, image,
        valid_mask[0])), pairing)

    odd_tile = (tile % 2) == 1
    above = jnp.where(odd_tile, got_even[rows - HALO:], got_odd[rows - HALO:])
    below = jnp.where(odd_tile, got_odd[:HALO], got_even[:HALO])
    own = jnp.concatenate([above, image, below, jnp.zeros((RAW_ROWS - rows - 2 * HALO, width), f32)], 0)
    even = lax.ppermute(own, "sec", pairs_even(sections))
    odd = lax.ppermute(own, "sec", pairs_odd(sections))
    packed = pl.pallas_call(
        own_features,
        out_shape=shape((WIDTH // WIN, 2, DEEP, WIDTH), bf16),
        in_specs=[VMEM] * 6, out_specs=VMEM,
        scratch_shapes=scratch(24, 18, 32) + [pltpu.VMEM((2, 2, (BLK + 2 * JOINT - 1) * C, WIDTH), bf16)],
        name="own_features", **params(5 * 10**9, 10**7),
    )(own, t1, t2, t3, spread, order)
    result = pl.pallas_call(
        correlate,
        out_shape=shape((8, SHIFTS * SHIFTS), f32),
        in_specs=[VMEM] * 11, out_specs=VMEM,
        scratch_shapes=scratch(32, 26, 48) + [
            pltpu.VMEM(((BLK + 2 * RADIUS) * C, WIDTH), f32),
            pltpu.VMEM((2, WIDTH + 2 * RADIUS, (BLK + 2 * RADIUS + JOINT) * C), bf16),
        ],
        name="correlate", **params(10**10, 10**7),
    )(choice, scale, own, even, odd, t1, t2, t3, spread, order, packed)
    return result[None, None]


def solution(mesh):
    placed = (
        P(("groups", "sec"), "tile", None),
        P(("groups", "sec")),
        P(("groups", "sec"), "tile", None),
        P(),
        P(),
        P(),
    )
    return jax.shard_map(
        body,
        mesh=mesh,
        in_specs=placed,
        out_specs=P(("groups", "sec"), "tile", None, None),
        check_vma=False,
    )
```

```python
import jax
import jax.numpy as jnp
import numpy as np
from jax import lax
from jax.experimental import pallas as pl
from jax.experimental.pallas import tpu as pltpu
from jax.sharding import PartitionSpec as P

LAYERS = 3
BLK = 32
RADIUS = 8
C = 32
SHIFTS = 2 * RADIUS + 1
HALO = RADIUS + LAYERS
RAW_ROWS = 64
LANES = 128
WIDTH = 256
WIN = 64
SPAN = WIN + 2 * RADIUS
JOINT = 4
STEPS = 5
DEEP = (BLK + JOINT) * C
BAND = 24
STREAMS = ((1, 2), (None, 0), (0, 1), (2, None))
FORMS = ((1, 0), (2, 1), (0, None), (None, 2))
bf16 = jnp.bfloat16
f32 = jnp.float32


def pairs_even(n):
    return [(i, i ^ 1) for i in range(n) if (i ^ 1) < n]


def pairs_odd(n):
    return [(i, ((i + 1) ^ 1) - 1) for i in range(n) if 0 <= ((i + 1) ^ 1) - 1 < n]


def split(value):
    high = value.astype(bf16)
    return high, (value - high.astype(f32)).astype(bf16)


def dot(left, right):
    return jnp.dot(left, right, preferred_element_type=f32)


def iota(shape, axis):
    return lax.broadcasted_iota(jnp.int32, shape, axis)


def prepare(later_hbm, first_hbm, bias_hbm, image_hbm, mask_hbm, pair_ref,
            t1, t2, t3, spread, order, image, scale, choice,
            later_ref, first_ref, bias_ref, mask_ref, arrived):
    copies = [
        pltpu.make_async_copy(source, target, arrived.at[i])
        for i, (source, target) in enumerate((
            (later_hbm, later_ref), (first_hbm, first_ref), (bias_hbm, bias_ref), (image_hbm, image),
            (mask_hbm, mask_ref)))
    ]
    for copy in copies:
        copy.start()
    row, col = iota((WIDTH, WIDTH), 0), iota((WIDTH, WIDTH), 1)
    order[0:WIDTH, :] = jnp.where(row == 2 * (col % LANES) + col // LANES, 1.0, 0.0).astype(bf16)
    order[WIDTH:, :] = jnp.where(col == 2 * (row % LANES) + row // LANES, 1.0, 0.0).astype(bf16)
    for copy in copies:
        copy.wait()
    section, pair = lax.axis_index("sec"), pair_ref[0]
    which = jnp.where(pair == section, 0, jnp.where(pair == (section ^ 1), 1, 2))
    choice[...] = jnp.broadcast_to(which, choice.shape)
    mask = jnp.concatenate([mask_ref[...].astype(f32), jnp.zeros((1, LANES - 8), f32)], 1)
    mask = jnp.transpose(jnp.broadcast_to(mask, (8, LANES)))[0:8, 0:1]
    scale[...] = jnp.broadcast_to(mask * np.float32(1.0 / np.sqrt(BLK * BLK * C)), scale.shape)
    nothing = jnp.zeros((C, C), f32)
    for layer, t in enumerate((t2, t3)):
        for stream, (even, odd) in enumerate(STREAMS):
            taps = []
            for ky in range(3):
                taps += [nothing if kx is None else later_ref[layer, ky, kx] for kx in (even, odd)]
            wide = jnp.concatenate(taps + [nothing, nothing], axis=1)
            for yo in range(2):
                high, low = split(pltpu.roll(wide, yo * 2 * C, 1) if yo else wide)
                rows = slice((yo * 4 + stream) * C, (yo * 4 + stream + 1) * C)
                t[0, rows, :] = high
                t[1, rows, :] = low
    shape = (16, 8 * 2 * C)
    offset = iota(shape, 0) - iota(shape, 1) // (2 * C)
    pieces = []
    for even, odd in FORMS:
        piece = jnp.zeros(shape, f32)
        for ky in range(3):
            pair = [jnp.zeros((1, C), f32) if kx is None else first_ref[ky, kx] for kx in (even, odd)]
            piece = jnp.where(offset == ky, jnp.broadcast_to(jnp.concatenate(pair * 8, 1), shape), piece)
        pieces.append(piece)
    pieces.append(jnp.zeros((64, 8 * 2 * C), f32))
    high, low = split(jnp.transpose(jnp.concatenate(pieces, 0)))
    t1[:, 0:64] = high[:, 0:64]
    t1[:, 64:128] = low[:, 0:64]
    t1[:, 128:192] = high[:, 0:64]
    b = jnp.concatenate([bias_ref[...], jnp.zeros((LAYERS, LANES - C), f32)], 1)
    b = jnp.transpose(jnp.concatenate([b, jnp.zeros((8 - LAYERS, LANES), f32)], 0))
    for layer in range(LAYERS):
        spread[layer] = jnp.broadcast_to(b[0:C, layer:layer + 1], (C, WIDTH))


def encode(image, starts, groups, ends, tile, tiles, t1, t2, t3, spread, order, raw, x1, x2, x3, emit):
    n1, n2, n3 = 8 * groups[0], 2 * groups[1], 2 * groups[2]
    h = image.astype(bf16)
    rest = image - h.astype(f32)
    m = rest.astype(bf16)
    l = (rest - m.astype(f32)).astype(bf16)
    apart = order[0:WIDTH, :]
    image = dot(jnp.concatenate([h, m, l], 1), jnp.concatenate([apart] * 3, 0))
    even, odd = image[:, :LANES], image[:, LANES:]
    col = iota((RAW_ROWS, LANES), 1)
    before = jnp.where(col == 0, 0.0, pltpu.roll(odd, 1, 1))
    after = jnp.where(col == LANES - 1, 0.0, pltpu.roll(even, LANES - 1, 1))
    for form, v in enumerate((even, odd, before, after)):
        raw[form] = jnp.concatenate([v[a:a + n1 + 8] for a in starts], 1)
    lane = iota((C, WIDTH), 1) % LANES
    twice = lambda v: jnp.concatenate([v, v], 0)

    def put(x, row, value):
        high, low = split(value)
        x[0, row * 2 * C:(row + 1) * 2 * C, :] = high
        x[1, row * 2 * C:(row + 1) * 2 * C, :] = low

    def outside(x, top, end, rows):
        @pl.when(tile == 0)
        def _():
            x[:, 0:top * 2 * C, 0:LANES] = jnp.zeros((2, top * 2 * C, LANES), bf16)

        @pl.when(tile == tiles - 1)
        def _():
            x[:, end * 2 * C:rows * 2 * C, LANES:] = jnp.zeros((2, (rows - end) * 2 * C, LANES), bf16)

    def shifted(v, by, blank):
        v = jnp.concatenate([pltpu.roll(v[:, i:i + LANES], by, 1) for i in range(0, WIDTH, LANES)], 1)
        return jnp.where(lane == blank, 0.0, v)

    def conv(t, x, step, bias):
        rows = slice(step * 4 * C, (step * 4 + 8) * C)
        th, tl, xh, xl = t[0], t[1], x[0, rows, :], x[1, rows, :]
        r = dot(jnp.concatenate([th, tl, th], 1), jnp.concatenate([xh, xh, xl], 0))
        for yo in range(2):
            a, b, c, d = (r[(yo * 4 + i) * C:(yo * 4 + i + 1) * C] for i in range(4))
            yield 2 * step + yo, a + shifted(b, 1, 0) + bias, c + shifted(d, LANES - 1, LANES - 1) + bias

    for g in range(groups[0]):
        high, low = split(jnp.concatenate([raw[form, 8 * g:8 * g + 16, :] for form in range(4)], 0))
        r = dot(t1[...], jnp.concatenate([high, high, low], 0))
        for yo in range(8):
            put(x1, 8 * g + yo, jnp.tanh(r[yo * 2 * C:(yo + 1) * 2 * C] + twice(spread[0])))
    outside(x1, ends[0], ends[1], n1)
    for step in range(groups[1]):
        for row, a, b in conv(t2, x1, step, spread[1]):
            put(x2, row, jnp.tanh(jnp.concatenate([a, b], 0)))
    outside(x2, ends[2], ends[3], n2)
    for step in range(groups[2]):
        for row, a, b in conv(t3, x2, step, spread[2]):
            for run in range(2):
                rows = slice((run * n3 + row) * C, (run * n3 + row + 1) * C)
                for parity, v in enumerate((a, b)):
                    half = v[:, run * LANES:(run + 1) * LANES]
                    if x3 is None:
                        emit(run * n3 + row, parity, half)
                        continue
                    high, low = split(half)
                    x3[rows, parity * LANES:(parity + 1) * LANES] = high
                    x3[rows, WIDTH + parity * LANES:WIDTH + (parity + 1) * LANES] = low
    if x3 is None:
        return
    together = jnp.concatenate([order[WIDTH:, :]] * 2, 0)
    for row in range(0, 2 * n3, 16):
        r = dot(x3[row * C:(row + 16) * C, :], together)
        for i in range(16):
            emit(row + i, r[i * C:(i + 1) * C])


def own_features(image_ref, t1, t2, t3, spread, order, kept, raw, x1, x2, x3):
    tile, tiles = lax.axis_index("tile"), lax.axis_size("tile")
    pad = JOINT - 1
    kept[:, :, 0:pad * C, :] = jnp.zeros((2, 2, pad * C, WIDTH), bf16)
    kept[:, :, (pad + BLK) * C:, :] = jnp.zeros((2, 2, JOINT * C, WIDTH), bf16)

    def emit(row, value):
        turned = [pltpu.roll(value[:, i:i + LANES], WIN, 1) for i in range(0, WIDTH, LANES)]
        rows = slice((row + pad) * C, (row + pad + 1) * C)
        for form, v in enumerate((value, jnp.concatenate(turned, 1))):
            kept[form, 0, rows, :], kept[form, 1, rows, :] = split(v)

    encode(image_ref[...], (8, 24), (3, 9, 8), (2, 18, 1, 17), tile, tiles,
           t1, t2, t3, spread, order, raw, x1, x2, x3, emit)


def joined(kept, w, part):
    left = iota((C, LANES), 1) < WIN
    half = slice((w // 2) * LANES, (w // 2 + 1) * LANES)
    rows = []
    for y in range(BLK + JOINT):
        at = y + JOINT - 1
        cols = []
        for g in (0, 2):
            a = kept[w % 2, part, (at - g) * C:(at - g + 1) * C, half]
            b = kept[1 - w % 2, part, (at - g - 1) * C:(at - g) * C, half]
            cols.append(jnp.where(left, a, b))
        rows.append(jnp.concatenate(cols, 1))
    return jnp.concatenate(rows, 0)


def correlate(choice, scale, own_ref, even_ref, odd_ref, t1, t2, t3, spread, order, kept, out_ref,
              raw, x1, x2, feats, mixed, turned):
    tile, tiles = lax.axis_index("tile"), lax.axis_size("tile")
    which = choice[...]
    image = jnp.where(which == 0, own_ref[...], jnp.where(which == 1, even_ref[...], odd_ref[...]))

    def emit(row, parity, half):
        feats[parity, row * C:(row + 1) * C, :] = half

    encode(image, (0, 24), (4, 13, 12), (10, 18, 9, 17), tile, tiles,
           t1, t2, t3, spread, order, raw, x1, x2, None, emit)

    @pl.when(tile == 0)
    def _():
        feats[:, 0:RADIUS * C, :] = jnp.zeros((2, RADIUS * C, LANES), f32)

    @pl.when(tile == tiles - 1)
    def _():
        feats[:, (BLK + RADIUS) * C:, :] = jnp.zeros((2, RADIUS * C, LANES), f32)

    border = jnp.zeros((RADIUS, LANES), f32)
    turned[:, :, (BLK + 2 * RADIUS) * C:] = jnp.zeros((2, WIDTH + 2 * RADIUS, JOINT * C), bf16)
    for q in range((BLK + 2 * RADIUS) * C // LANES):
        cols = slice(q * LANES, (q + 1) * LANES)
        for parity in range(2):
            mixed[q, pl.ds(RADIUS + parity, LANES, stride=2), :] = jnp.transpose(feats[parity, cols, :])
        mixed[q, 0:RADIUS, :] = border
        mixed[q, RADIUS + WIDTH:, :] = border
        turned[0, :, cols], turned[1, :, cols] = split(mixed[q])

    lane8, sub8 = iota((8, LANES), 1), iota((8, LANES), 0)
    eighth = (iota((8, WIDTH), 1) % WIN) // 8
    sums = [[None] * 8 for _ in range(JOINT)]
    for w in range(WIDTH // WIN):
        rows = slice(w * WIN, w * WIN + SPAN)
        lefts = []
        for j in range(STEPS):
            cols = slice(j * JOINT * C, j * JOINT * C + DEEP)
            high, low = turned[0, rows, cols], turned[1, rows, cols]
            lefts.append(jnp.concatenate([high, low, high], 1))
        high, low = joined(kept, w, 0), joined(kept, w, 1)
        right = jnp.concatenate([high, high, low], 0)
        p = dot(jnp.concatenate(lefts, 0), right)
        bands = []
        for j in range(STEPS):
            for k in range(3):
                band = None
                for m in range(8):
                    start = j * SPAN + 8 * (m + k)
                    v = p[start:start + 8, :]
                    band = v if band is None else jnp.where(eighth == m, v, band)
                bands.append(band)
        bands.append(jnp.zeros((8, WIDTH), f32))
        flat = jnp.transpose(jnp.concatenate(bands, 0))
        for g in range(JOINT):
            for side in range(2):
                at = g * WIN + side * BLK
                v = flat[at:at + 8] + flat[at + 8:at + 16] + flat[at + 16:at + 24] + flat[at + 24:at + 32]
                for bit in (1, 2, 4):
                    v = jnp.where((sub8 & bit) != 0, pltpu.roll(v, LANES - bit, 1), v)
                sums[g][2 * w + side] = jnp.sum(v, axis=0, keepdims=True)
    total = jnp.zeros((8, 3 * LANES), f32)
    lane = iota((8, 3 * LANES), 1)
    for g in range(JOINT):
        d = jnp.concatenate(sums[g], 0)
        d = jnp.concatenate([d, jnp.zeros((8, 2 * LANES), f32)], 1)
        for j in range(STEPS):
            dy = JOINT * j + g
            if dy < SHIFTS:
                shift = (SHIFTS * dy - BAND * j) % (3 * LANES)
                here = (lane >= SHIFTS * dy) & (lane < SHIFTS * (dy + 1))
                total = jnp.where(here, pltpu.roll(d, shift, 1) if shift else d, total)
    total = total * scale[...]
    out_ref[...] = total[:, :SHIFTS * SHIFTS]


VMEM = pl.BlockSpec(memory_space=pltpu.VMEM)
HBM = pl.BlockSpec(memory_space=pltpu.HBM)


def params(flops, moved, mib=40):
    return dict(
        compiler_params=pltpu.CompilerParams(vmem_limit_bytes=mib << 20),
        cost_estimate=pl.CostEstimate(flops=flops, bytes_accessed=moved, transcendentals=0),
    )


def scratch(rows1, rows2, rows3):
    return [
        pltpu.VMEM((4, rows1 + 8, WIDTH), f32),
        pltpu.VMEM((2, rows1 * 2 * C, WIDTH), bf16),
        pltpu.VMEM((2, rows2 * 2 * C, WIDTH), bf16),
        pltpu.VMEM((rows3 * C, 2 * WIDTH), bf16),
    ]


def body(raw_image, pairing, valid_mask, first_kernel, later_kernels, biases):
    tiles, sections = lax.axis_size("tile"), lax.axis_size("sec")
    tile = lax.axis_index("tile")
    image = raw_image[0]
    rows, width = image.shape
    shape = jax.ShapeDtypeStruct
    got_even = lax.ppermute(image, "tile", pairs_even(tiles))
    got_odd = lax.ppermute(image, "tile", pairs_odd(tiles))
    t1, t2, t3, spread, order, image, scale, choice = pl.pallas_call(
        prepare,
        out_shape=[shape((512, 192), bf16), shape((2, WIDTH, WIDTH), bf16), shape((2, WIDTH, WIDTH), bf16),
                   shape((LAYERS, C, WIDTH), f32), shape((2 * WIDTH, WIDTH), bf16), shape(image.shape, f32), shape((8, 3 * LANES), f32),
                   shape((RAW_ROWS, WIDTH), jnp.int32)],
        in_specs=[HBM] * 5 + [pl.BlockSpec(memory_space=pltpu.SMEM)], out_specs=[VMEM] * 8,
        scratch_shapes=[pltpu.VMEM((2, 3, 3, C, C), f32), pltpu.VMEM((3, 3, 1, C), f32),
                        pltpu.VMEM((LAYERS, C), f32), pltpu.VMEM((1, 8), jnp.int32),
                        pltpu.SemaphoreType.DMA((5,))],
        name="prepare", **params(10**6, 3 * 10**6),
    )(*(pltpu.with_memory_space_constraint(v, pltpu.HBM) for v in (
        jnp.transpose(later_kernels, (0, 3, 4, 1, 2)), jnp.transpose(first_kernel, (2, 3, 1, 0)), biases, image,
        valid_mask[0])), pairing)

    odd_tile = (tile % 2) == 1
    above = jnp.where(odd_tile, got_even[rows - HALO:], got_odd[rows - HALO:])
    below = jnp.where(odd_tile, got_odd[:HALO], got_even[:HALO])
    own = jnp.concatenate([above, image, below, jnp.zeros((RAW_ROWS - rows - 2 * HALO, width), f32)], 0)
    even = lax.ppermute(own, "sec", pairs_even(sections))
    odd = lax.ppermute(own, "sec", pairs_odd(sections))
    kept = pl.pallas_call(
        own_features,
        out_shape=shape((2, 2, (BLK + 2 * JOINT - 1) * C, WIDTH), bf16),
        in_specs=[VMEM] * 6, out_specs=VMEM,
        scratch_shapes=scratch(24, 18, 32),
        name="own_features", **params(5 * 10**9, 10**7),
    )(own, t1, t2, t3, spread, order)
    result = pl.pallas_call(
        correlate,
        out_shape=shape((8, SHIFTS * SHIFTS), f32),
        in_specs=[VMEM] * 11, out_specs=VMEM,
        scratch_shapes=scratch(32, 26, 0)[:3] + [
            pltpu.VMEM((2, (BLK + 2 * RADIUS) * C, LANES), f32),
            pltpu.VMEM(((BLK + 2 * RADIUS) * C // LANES, WIDTH + 2 * RADIUS, LANES), f32),
            pltpu.VMEM((2, WIDTH + 2 * RADIUS, (BLK + 2 * RADIUS + JOINT) * C), bf16),
        ],
        name="correlate", **params(10**10, 10**7),
    )(choice, scale, own, even, odd, t1, t2, t3, spread, order, kept)
    return result[None, None]


def solution(mesh):
    placed = (
        P(("groups", "sec"), "tile", None),
        P(("groups", "sec")),
        P(("groups", "sec"), "tile", None),
        P(),
        P(),
        P(),
    )
    return jax.shard_map(
        body,
        mesh=mesh,
        in_specs=placed,
        out_specs=P(("groups", "sec"), "tile", None, None),
        check_vma=False,
    )
```

```python
import jax
import jax.numpy as jnp
import numpy as np
from jax import lax
from jax.experimental import pallas as pl
from jax.experimental.pallas import tpu as pltpu
from jax.sharding import PartitionSpec as P

LAYERS = 3
BLK = 32
RADIUS = 8
C = 32
SHIFTS = 2 * RADIUS + 1
HALO = RADIUS + LAYERS
RAW_ROWS = 64
LANES = 128
WIDTH = 256
WIN = 64
SPAN = WIN + 2 * RADIUS
JOINT = 4
STEPS = 5
DEEP = (BLK + JOINT) * C
BAND = 24
STREAMS = ((1, 2), (None, 0), (0, 1), (2, None))
FORMS = ((1, 0), (2, 1), (0, None), (None, 2))
bf16 = jnp.bfloat16
f32 = jnp.float32


def pairs_even(n):
    return [(i, i ^ 1) for i in range(n) if (i ^ 1) < n]


def pairs_odd(n):
    return [(i, ((i + 1) ^ 1) - 1) for i in range(n) if 0 <= ((i + 1) ^ 1) - 1 < n]


def split(value):
    high = value.astype(bf16)
    return high, (value - high.astype(f32)).astype(bf16)


def dot(left, right):
    return jnp.dot(left, right, preferred_element_type=f32)


def iota(shape, axis):
    return lax.broadcasted_iota(jnp.int32, shape, axis)


def prepare(later_hbm, first_hbm, bias_hbm, image_hbm, mask_hbm, pair_ref,
            t1, t2, t3, spread, order, image, scale, choice,
            later_ref, first_ref, bias_ref, mask_ref, arrived):
    copies = [
        pltpu.make_async_copy(source, target, arrived.at[i])
        for i, (source, target) in enumerate((
            (later_hbm, later_ref), (first_hbm, first_ref), (bias_hbm, bias_ref), (image_hbm, image),
            (mask_hbm, mask_ref)))
    ]
    for copy in copies:
        copy.start()
    row, col = iota((WIDTH, WIDTH), 0), iota((WIDTH, WIDTH), 1)
    order[0:WIDTH, :] = jnp.where(row == 2 * (col % LANES) + col // LANES, 1.0, 0.0).astype(bf16)
    order[WIDTH:, :] = jnp.where(col == 2 * (row % LANES) + row // LANES, 1.0, 0.0).astype(bf16)
    for copy in copies:
        copy.wait()
    section, pair = lax.axis_index("sec"), pair_ref[0]
    which = jnp.where(pair == section, 0, jnp.where(pair == (section ^ 1), 1, 2))
    choice[...] = jnp.broadcast_to(which, choice.shape)
    mask = jnp.concatenate([mask_ref[...].astype(f32), jnp.zeros((1, LANES - 8), f32)], 1)
    mask = jnp.transpose(jnp.broadcast_to(mask, (8, LANES)))[0:8, 0:1]
    scale[...] = jnp.broadcast_to(mask * np.float32(1.0 / np.sqrt(BLK * BLK * C)), scale.shape)
    nothing = jnp.zeros((C, C), f32)
    for layer, t in enumerate((t2, t3)):
        for stream, (even, odd) in enumerate(STREAMS):
            taps = []
            for ky in range(3):
                taps += [nothing if kx is None else later_ref[layer, ky, kx] for kx in (even, odd)]
            wide = jnp.concatenate(taps + [nothing, nothing], axis=1)
            for yo in range(2):
                high, low = split(pltpu.roll(wide, yo * 2 * C, 1) if yo else wide)
                rows = slice((yo * 4 + stream) * C, (yo * 4 + stream + 1) * C)
                t[0, rows, :] = high
                t[1, rows, :] = low
    shape = (16, 8 * 2 * C)
    offset = iota(shape, 0) - iota(shape, 1) // (2 * C)
    pieces = []
    for even, odd in FORMS:
        piece = jnp.zeros(shape, f32)
        for ky in range(3):
            pair = [jnp.zeros((1, C), f32) if kx is None else first_ref[ky, kx] for kx in (even, odd)]
            piece = jnp.where(offset == ky, jnp.broadcast_to(jnp.concatenate([jnp.concatenate(pair * 2, 1)] * 4, 1), shape), piece)
        pieces.append(piece)
    pieces.append(jnp.zeros((64, 8 * 2 * C), f32))
    high, low = split(jnp.transpose(jnp.concatenate(pieces, 0)))
    t1[:, 0:64] = high[:, 0:64]
    t1[:, 64:128] = low[:, 0:64]
    t1[:, 128:192] = high[:, 0:64]
    b = jnp.concatenate([bias_ref[...], jnp.zeros((LAYERS, LANES - C), f32)], 1)
    b = jnp.transpose(jnp.concatenate([b, jnp.zeros((8 - LAYERS, LANES), f32)], 0))
    for layer in range(LAYERS):
        spread[layer] = jnp.broadcast_to(b[0:C, layer:layer + 1], (C, WIDTH))


def encode(image, starts, groups, ends, tile, tiles, t1, t2, t3, spread, order, raw, x1, x2, x3, emit):
    n1, n2, n3 = groups[0], 2 * groups[1], 2 * groups[2]
    h = image.astype(bf16)
    rest = image - h.astype(f32)
    m = rest.astype(bf16)
    l = (rest - m.astype(f32)).astype(bf16)
    apart = order[0:WIDTH, :]
    image = dot(jnp.concatenate([h, m, l], 1), jnp.concatenate([apart] * 3, 0))
    even, odd = image[:, :LANES], image[:, LANES:]
    col = iota((RAW_ROWS, LANES), 1)
    before = jnp.where(col == 0, 0.0, pltpu.roll(odd, 1, 1))
    after = jnp.where(col == LANES - 1, 0.0, pltpu.roll(even, LANES - 1, 1))
    for form, v in enumerate((even, odd, before, after)):
        raw[form] = jnp.concatenate([v[a:a + raw.shape[1]] for a in starts], 1)
    lane = iota((C, WIDTH), 1) % LANES
    twice = lambda v: jnp.concatenate([v, v], 0)

    def put(x, row, value):
        high, low = split(value)
        x[0, row * 2 * C:(row + 1) * 2 * C, :] = high
        x[1, row * 2 * C:(row + 1) * 2 * C, :] = low

    def outside(x, top, end, rows):
        @pl.when(tile == 0)
        def _():
            x[:, 0:top * 2 * C, 0:LANES] = jnp.zeros((2, top * 2 * C, LANES), bf16)

        @pl.when(tile == tiles - 1)
        def _():
            x[:, end * 2 * C:rows * 2 * C, LANES:] = jnp.zeros((2, (rows - end) * 2 * C, LANES), bf16)

    def shifted(v, by, blank):
        v = jnp.concatenate([pltpu.roll(v[:, i:i + LANES], by, 1) for i in range(0, WIDTH, LANES)], 1)
        return jnp.where(lane == blank, 0.0, v)

    def conv(t, x, step, bias):
        rows = slice(step * 4 * C, (step * 4 + 8) * C)
        th, tl, xh, xl = t[0], t[1], x[0, rows, :], x[1, rows, :]
        r = dot(jnp.concatenate([th, tl, th], 1), jnp.concatenate([xh, xh, xl], 0))
        for yo in range(2):
            a, b, c, d = (r[(yo * 4 + i) * C:(yo * 4 + i + 1) * C] for i in range(4))
            yield 2 * step + yo, a + shifted(b, 1, 0) + bias, c + shifted(d, LANES - 1, LANES - 1) + bias

    for g in range((n1 + 7) // 8):
        count = min(8, n1 - 8 * g)
        high, low = split(jnp.concatenate([raw[form, 8 * g:8 * g + 16, :] for form in range(4)], 0))
        r = dot(t1[0:count * 2 * C, :], jnp.concatenate([high, high, low], 0))
        for yo in range(count):
            put(x1, 8 * g + yo, jnp.tanh(r[yo * 2 * C:(yo + 1) * 2 * C] + twice(spread[0])))
    outside(x1, ends[0], ends[1], n1)
    for step in range(groups[1]):
        for row, a, b in conv(t2, x1, step, spread[1]):
            put(x2, row, jnp.tanh(jnp.concatenate([a, b], 0)))
    outside(x2, ends[2], ends[3], n2)
    for step in range(groups[2]):
        for row, a, b in conv(t3, x2, step, spread[2]):
            for run in range(2):
                rows = slice((run * n3 + row) * C, (run * n3 + row + 1) * C)
                for parity, v in enumerate((a, b)):
                    half = v[:, run * LANES:(run + 1) * LANES]
                    if x3 is None:
                        emit(run * n3 + row, parity, half)
                        continue
                    high, low = split(half)
                    x3[rows, parity * LANES:(parity + 1) * LANES] = high
                    x3[rows, WIDTH + parity * LANES:WIDTH + (parity + 1) * LANES] = low
    if x3 is None:
        return
    together = jnp.concatenate([order[WIDTH:, :]] * 2, 0)
    for row in range(0, 2 * n3, 16):
        r = dot(x3[row * C:(row + 16) * C, :], together)
        for i in range(16):
            emit(row + i, r[i * C:(i + 1) * C])


def own_features(image_ref, t1, t2, t3, spread, order, kept, raw, x1, x2, x3):
    tile, tiles = lax.axis_index("tile"), lax.axis_size("tile")
    pad = JOINT - 1
    kept[:, :, 0:pad * C, :] = jnp.zeros((2, 2, pad * C, WIDTH), bf16)
    kept[:, :, (pad + BLK) * C:, :] = jnp.zeros((2, 2, JOINT * C, WIDTH), bf16)

    def emit(row, value):
        turned = [pltpu.roll(value[:, i:i + LANES], WIN, 1) for i in range(0, WIDTH, LANES)]
        rows = slice((row + pad) * C, (row + pad + 1) * C)
        for form, v in enumerate((value, jnp.concatenate(turned, 1))):
            kept[form, 0, rows, :], kept[form, 1, rows, :] = split(v)

    encode(image_ref[...], (8, 24), (20, 9, 8), (2, 18, 1, 17), tile, tiles,
           t1, t2, t3, spread, order, raw, x1, x2, x3, emit)


def joined(kept, w, part):
    left = iota((C, LANES), 1) < WIN
    half = slice((w // 2) * LANES, (w // 2 + 1) * LANES)
    rows = []
    for y in range(BLK + JOINT):
        at = y + JOINT - 1
        cols = []
        for g in (0, 2):
            a = kept[w % 2, part, (at - g) * C:(at - g + 1) * C, half]
            b = kept[1 - w % 2, part, (at - g - 1) * C:(at - g) * C, half]
            cols.append(jnp.where(left, a, b))
        rows.append(jnp.concatenate(cols, 1))
    return jnp.concatenate(rows, 0)


def correlate(choice, scale, own_ref, even_ref, odd_ref, t1, t2, t3, spread, order, kept, out_ref,
              raw, x1, x2, feats, mixed, turned):
    tile, tiles = lax.axis_index("tile"), lax.axis_size("tile")
    which = choice[...]
    image = jnp.where(which == 0, own_ref[...], jnp.where(which == 1, even_ref[...], odd_ref[...]))

    border = jnp.zeros((RADIUS, LANES), f32)
    deep = (BLK + 2 * RADIUS) * C
    turned[:, :, deep:] = jnp.zeros((2, WIDTH + 2 * RADIUS, JOINT * C), bf16)

    def emit(row, parity, half):
        feats[parity, row * C:(row + 1) * C, :] = half
        if row % 4 < 3 or parity == 0:
            return
        q = row // 4
        cols = slice(q * LANES, (q + 1) * LANES)
        for p in range(2):
            mixed[q, pl.ds(RADIUS + p, LANES, stride=2), :] = jnp.transpose(feats[p, cols, :])
        mixed[q, 0:RADIUS, :] = border
        mixed[q, RADIUS + WIDTH:, :] = border
        turned[0, :, cols], turned[1, :, cols] = split(mixed[q])

    encode(image, (0, 24), (28, 13, 12), (10, 18, 9, 17), tile, tiles,
           t1, t2, t3, spread, order, raw, x1, x2, None, emit)
    beyond = jnp.zeros((2, WIDTH + 2 * RADIUS, RADIUS * C), bf16)

    @pl.when(tile == 0)
    def _():
        turned[:, :, 0:RADIUS * C] = beyond

    @pl.when(tile == tiles - 1)
    def _():
        turned[:, :, deep - RADIUS * C:deep] = beyond

    lane8, sub8 = iota((8, LANES), 1), iota((8, LANES), 0)
    eighth = (iota((8, WIDTH), 1) % WIN) // 8
    sums = [[None] * 8 for _ in range(JOINT)]
    for w in range(WIDTH // WIN):
        rows = slice(w * WIN, w * WIN + SPAN)
        lefts = []
        for j in range(STEPS):
            cols = slice(j * JOINT * C, j * JOINT * C + DEEP)
            high, low = turned[0, rows, cols], turned[1, rows, cols]
            lefts.append(jnp.concatenate([high, low, high], 1))
        high, low = joined(kept, w, 0), joined(kept, w, 1)
        right = jnp.concatenate([high, high, low], 0)
        p = dot(jnp.concatenate(lefts, 0), right)
        bands = []
        for j in range(STEPS):
            for k in range(3):
                band = None
                for m in range(8):
                    start = j * SPAN + 8 * (m + k)
                    v = p[start:start + 8, :]
                    band = v if band is None else jnp.where(eighth == m, v, band)
                bands.append(band)
        bands.append(jnp.zeros((8, WIDTH), f32))
        flat = jnp.transpose(jnp.concatenate(bands, 0))
        for g in range(JOINT):
            for side in range(2):
                at = g * WIN + side * BLK
                v = flat[at:at + 8] + flat[at + 8:at + 16] + flat[at + 16:at + 24] + flat[at + 24:at + 32]
                for bit in (1, 2, 4):
                    v = jnp.where((sub8 & bit) != 0, pltpu.roll(v, LANES - bit, 1), v)
                sums[g][2 * w + side] = jnp.sum(v, axis=0, keepdims=True)
    total = jnp.zeros((8, 3 * LANES), f32)
    lane = iota((8, 3 * LANES), 1)
    for g in range(JOINT):
        d = jnp.concatenate(sums[g], 0)
        d = jnp.concatenate([d, jnp.zeros((8, 2 * LANES), f32)], 1)
        for j in range(STEPS):
            dy = JOINT * j + g
            if dy < SHIFTS:
                shift = (SHIFTS * dy - BAND * j) % (3 * LANES)
                here = (lane >= SHIFTS * dy) & (lane < SHIFTS * (dy + 1))
                total = jnp.where(here, pltpu.roll(d, shift, 1) if shift else d, total)
    total = total * scale[...]
    out_ref[...] = total[:, :SHIFTS * SHIFTS]


VMEM = pl.BlockSpec(memory_space=pltpu.VMEM)
HBM = pl.BlockSpec(memory_space=pltpu.HBM)


def params(flops, moved, mib=40):
    return dict(
        compiler_params=pltpu.CompilerParams(vmem_limit_bytes=mib << 20),
        cost_estimate=pl.CostEstimate(flops=flops, bytes_accessed=moved, transcendentals=0),
    )


def scratch(rows1, rows2, rows3):
    return [
        pltpu.VMEM((4, (rows1 + 7) // 8 * 8 + 8, WIDTH), f32),
        pltpu.VMEM((2, rows1 * 2 * C, WIDTH), bf16),
        pltpu.VMEM((2, rows2 * 2 * C, WIDTH), bf16),
        pltpu.VMEM((rows3 * C, 2 * WIDTH), bf16),
    ]


def body(raw_image, pairing, valid_mask, first_kernel, later_kernels, biases):
    tiles, sections = lax.axis_size("tile"), lax.axis_size("sec")
    tile = lax.axis_index("tile")
    image = raw_image[0]
    rows, width = image.shape
    shape = jax.ShapeDtypeStruct
    got_even = lax.ppermute(image, "tile", pairs_even(tiles))
    got_odd = lax.ppermute(image, "tile", pairs_odd(tiles))
    t1, t2, t3, spread, order, image, scale, choice = pl.pallas_call(
        prepare,
        out_shape=[shape((512, 192), bf16), shape((2, WIDTH, WIDTH), bf16), shape((2, WIDTH, WIDTH), bf16),
                   shape((LAYERS, C, WIDTH), f32), shape((2 * WIDTH, WIDTH), bf16), shape(image.shape, f32), shape((8, 3 * LANES), f32),
                   shape((RAW_ROWS, WIDTH), jnp.int32)],
        in_specs=[HBM] * 5 + [pl.BlockSpec(memory_space=pltpu.SMEM)], out_specs=[VMEM] * 8,
        scratch_shapes=[pltpu.VMEM((2, 3, 3, C, C), f32), pltpu.VMEM((3, 3, 1, C), f32),
                        pltpu.VMEM((LAYERS, C), f32), pltpu.VMEM((1, 8), jnp.int32),
                        pltpu.SemaphoreType.DMA((5,))],
        name="prepare", **params(10**6, 3 * 10**6),
    )(*(pltpu.with_memory_space_constraint(v, pltpu.HBM) for v in (
        jnp.transpose(later_kernels, (0, 3, 4, 1, 2)), jnp.transpose(first_kernel, (2, 3, 1, 0)), biases, image,
        valid_mask[0])), pairing)

    even_tile = (tile % 2) == 0
    below = jnp.where(even_tile, got_even[:HALO], got_odd[:HALO])
    above = jnp.where(even_tile, got_odd[rows - HALO:], got_even[rows - HALO:])
    own = jnp.concatenate([above, image, below, jnp.zeros((RAW_ROWS - rows - 2 * HALO, width), f32)], 0)
    even = lax.ppermute(own, "sec", pairs_even(sections))
    odd = lax.ppermute(own, "sec", pairs_odd(sections))
    kept = pl.pallas_call(
        own_features,
        out_shape=shape((2, 2, (BLK + 2 * JOINT - 1) * C, WIDTH), bf16),
        in_specs=[VMEM] * 6, out_specs=VMEM,
        scratch_shapes=scratch(20, 18, 32),
        name="own_features", **params(5 * 10**9, 10**7),
    )(own, t1, t2, t3, spread, order)
    result = pl.pallas_call(
        correlate,
        out_shape=shape((8, SHIFTS * SHIFTS), f32),
        in_specs=[VMEM] * 11, out_specs=VMEM,
        scratch_shapes=scratch(28, 26, 0)[:3] + [
            pltpu.VMEM((2, (BLK + 2 * RADIUS) * C, LANES), f32),
            pltpu.VMEM(((BLK + 2 * RADIUS) * C // LANES, WIDTH + 2 * RADIUS, LANES), f32),
            pltpu.VMEM((2, WIDTH + 2 * RADIUS, (BLK + 2 * RADIUS + JOINT) * C), bf16),
        ],
        name="correlate", **params(10**10, 10**7),
    )(choice, scale, own, even, odd, t1, t2, t3, spread, order, kept)
    return result[None, None]


def solution(mesh):
    placed = (
        P(("groups", "sec"), "tile", None),
        P(("groups", "sec")),
        P(("groups", "sec"), "tile", None),
        P(),
        P(),
        P(),
    )
    return jax.shard_map(
        body,
        mesh=mesh,
        in_specs=placed,
        out_specs=P(("groups", "sec"), "tile", None, None),
        check_vma=False,
    )
```
